128 devices in a mesh: brick: 64 (over z_lo, x, y, core), vec: 2 (over z_hi).
Axes of the slice: x: 4, y: 4, z: 4 (z_hi: 2, z_lo: 2; z = z_hi * 2 + z_lo), core: 2. Of those that a mesh axis runs over, the one named last changes fastest.
Arguments:
- levels: int32 [12, 2048, 16, 128], P(None, 'brick'), may hold values from 0 to 255
- start_block: int32 [16, 2048, 16, 128], P('vec', 'brick'), may hold values from -8 to 8
Outputs:
- alpha_blocks: float32 [1, 16, 16], replicated
- beta_blocks: float32 [1, 16, 16], replicated
- basis: float32 [16, 2048, 16, 128], P('vec', 'brick')
The draws below stay inside these ranges and needn't reach their ends.
All inputs are finite; a program needn't handle non-finite values.
Results may differ from the reference program's by a relative error of at most 0.00026.
Values sent between devices are 32-bit elements; how exact they have to be, the bound alone decides.
No kernel may reach another device: no remote copies, remote signals or barrier semaphores. Data moves between devices by JAX's collectives and lax.ppermute only.
A program may use at most 128 MiB of HBM per device.

```python
import math
import jax
import jax.numpy as jnp
from jax import lax

BLOCK = 16
CHANNELS = 12
STEPS = 1
NY = 16
NZ = 128
NX = 2048
VOXELS = 4194304


def plant(values, key, smallest, high):
    shape = values.shape
    place = [jax.random.randint(jax.random.fold_in(key, axis), (), 0, shape[axis]) for axis in range(len(shape))]
    values = values.at[tuple(place)].set(smallest)
    longest = shape.index(max(shape))
    place[longest] = (place[longest] + 1) % shape[longest]
    return values.at[tuple(place)].set(high)


def setup_inputs(seed: int = 0) -> dict:
    keys = jax.random.split(jax.random.key(seed), 3)
    levels = plant(jax.random.randint(keys[0], (CHANNELS, NX, NY, NZ), 0, 256), jax.random.fold_in(keys[0], 1), 0, 255).astype(jnp.int32)
    start_block = plant(jax.random.randint(keys[1], (BLOCK, NX, NY, NZ), -8, 9), jax.random.fold_in(keys[1], 1), -8, 8).astype(jnp.int32)
    return dict(levels=levels, start_block=start_block)


offsets_cube = (1, 3, 9, 27)
highest = lax.Precision.HIGHEST

def forward_take(field_in, offset, axis_dim):
    length_dim = field_in.shape[axis_dim]
    widths = [(0, 0)] * field_in.ndim
    widths[axis_dim] = (0, offset)
    return lax.slice_in_dim(jnp.pad(field_in, widths), offset, offset + length_dim, axis=axis_dim)

def backward_put(field_in, offset, axis_dim):
    length_dim = field_in.shape[axis_dim]
    widths = [(0, 0)] * field_in.ndim
    widths[axis_dim] = (offset, 0)
    return lax.slice_in_dim(jnp.pad(field_in, widths), 0, length_dim, axis=axis_dim)

def affinity_apply(field_in, weights):
    result = jnp.zeros_like(field_in)
    for axis_dim in range(3):
        for position, offset in enumerate(offsets_cube):
            channel = weights[4 * axis_dim + position]
            result = result + channel * forward_take(field_in, offset, axis_dim) + backward_put(channel * field_in, offset, axis_dim)
    return result

def inner_of(left_rows, right_rows):
    return jnp.einsum('in,jn->ij', left_rows, right_rows, precision=highest)

def reference(levels, start_block):
    weights = (levels.astype(jnp.float32) + 0.5) / 256.0
    degree = affinity_apply(jnp.ones(levels.shape[1:], jnp.float32), weights) + 1.0
    inv_root = lax.rsqrt(degree)

    def half_step(column):
        return 0.5 * (column + inv_root * affinity_apply(inv_root * column, weights))

    def filtered(column):
        return half_step(half_step(column))
    shape_grid = start_block.shape
    start_work = start_block.astype(jnp.float32).reshape(BLOCK, -1)
    lower_factor = jnp.linalg.cholesky(inner_of(start_work, start_work))
    current = lax.linalg.triangular_solve(lower_factor, start_work, left_side=True, lower=True)
    known_rows = current
    alpha_list = []
    beta_list = []
    for sweep_index in range(STEPS):
        image_block = lax.map(filtered, current.reshape(shape_grid)).reshape(BLOCK, -1)
        coeffs = inner_of(image_block, known_rows)
        residual = image_block - jnp.einsum('ij,jn->in', coeffs, known_rows, precision=highest)
        gram_matrix = inner_of(residual, residual)
        lower_factor = jnp.linalg.cholesky(gram_matrix)
        following = lax.linalg.triangular_solve(lower_factor, residual, left_side=True, lower=True)
        alpha_list.append(coeffs[:, :BLOCK])
        beta_list.append(lower_factor)
        known_rows = jnp.concatenate([following, current], axis=0)
        current = following
    basis = current.reshape(shape_grid) * math.sqrt(VOXELS)
    return (jnp.stack(alpha_list), jnp.stack(beta_list), basis)
```

```python
import functools
import math

import jax
import jax.numpy as jnp
from jax import lax
from jax.experimental import pallas as pl
from jax.experimental.pallas import tpu as pltpu
from jax.sharding import PartitionSpec as P

offsets_cube = (1, 3, 9, 27)
deepest = 27
highest = lax.Precision.HIGHEST
chunk = 4
f32 = jnp.float32


ANY = pl.BlockSpec(memory_space=pl.ANY)
SMEM = pl.BlockSpec(memory_space=pltpu.SMEM)
VMEM = pl.BlockSpec(memory_space=pltpu.VMEM)


def params(mib):
    return pltpu.CompilerParams(vmem_limit_bytes=mib << 20)


def shift_rows(value, by):
    length = value.shape[-2]
    if abs(by) >= length:
        return jnp.zeros_like(value)
    rolled = pltpu.roll(value, (-by) % length, value.ndim - 2)
    row = lax.broadcasted_iota(jnp.int32, value.shape, value.ndim - 2) + by
    return jnp.where((row >= 0) & (row < length), rolled, 0.0)


def shift_lanes(value, by):
    length = value.shape[-1]
    if abs(by) >= length:
        return jnp.zeros_like(value)
    rolled = pltpu.roll(value, (-by) % length, value.ndim - 1)
    lane = lax.broadcasted_iota(jnp.int32, value.shape, value.ndim - 1) + by
    return jnp.where((lane >= 0) & (lane < length), rolled, 0.0)


def inverse_root(value):
    guess = lax.rsqrt(value)
    return guess * (1.5 - 0.5 * value * guess * guess)


def to_weight(level):
    return (level.astype(f32) + 0.5) / 256.0


def halo_start(position):
    return sum(offsets_cube[:position])


def degree_kernel(flag_ref, levels_ref, halo_ref, root_ref):
    planes = levels_ref.shape[1]
    inside_above = flag_ref[0].astype(f32)

    def plane(x, _):
        total = jnp.ones(levels_ref.shape[2:], f32)
        for position, offset in enumerate(offsets_cube):
            weight = to_weight(levels_ref[position, x])
            total = total + jnp.where(x + offset < planes, 1.0, inside_above) * weight
            own = to_weight(levels_ref[position, jnp.maximum(x - offset, 0)])
            base = halo_start(position)
            far = halo_ref[base + jnp.minimum(x, offset - 1)]
            total = total + jnp.where(x >= offset, own, far)
            for axis, shift in ((1, shift_rows), (2, shift_lanes)):
                weight = to_weight(levels_ref[4 * axis + position, x])
                ones = shift(jnp.ones_like(weight), offset)
                total = total + ones * weight + shift(weight, -offset)
        root_ref[x] = inverse_root(total)
        return 0

    lax.fori_loop(0, planes, plane, 0)


def weights_kernel(levels_ref, halo_ref, root_ref, above_ref, below_ref, out_ref):
    planes = levels_ref.shape[1]

    def plane(x, _):
        root = root_ref[x]
        half = 0.5 * root
        slot = 0
        for position, offset in enumerate(offsets_cube):
            ahead = jnp.where(
                x + offset < planes,
                root_ref[jnp.minimum(x + offset, planes - 1)],
                above_ref[jnp.maximum(x + offset - planes, 0)],
            )
            out_ref[slot, x] = to_weight(levels_ref[position, x]) * half * ahead
            back = jnp.maximum(x - offset, 0)
            base = halo_start(position)
            weight = jnp.where(
                x >= offset, to_weight(levels_ref[position, back]), halo_ref[base + jnp.minimum(x, offset - 1)]
            )
            behind = jnp.where(
                x >= offset, root_ref[back], below_ref[jnp.clip(deepest + x - offset, 0, deepest - 1)]
            )
            out_ref[slot + 1, x] = weight * half * behind
            slot += 2
        for axis, shift in ((1, shift_rows), (2, shift_lanes)):
            for position, offset in enumerate(offsets_cube):
                if offset >= root.shape[axis - 1]:
                    continue
                weight = to_weight(levels_ref[4 * axis + position, x])
                forward = weight * half * shift(root, offset)
                out_ref[slot, x] = forward
                out_ref[slot + 1, x] = shift(forward, -offset)
                slot += 2
        return 0

    lax.fori_loop(0, planes, plane, 0)


def terms_of(rows, lanes):
    found = [("x", o * s) for o in offsets_cube for s in (1, -1)]
    found += [("y", o * s) for o in offsets_cube if o < rows for s in (1, -1)]
    found += [("z", o * s) for o in offsets_cube if o < lanes for s in (1, -1)]
    return found


def filter_plane(ext_ref, weight_ref, x_local, x_plane, terms, rows, lanes):
    base = pl.multiple_of((x_plane + deepest) * rows, rows)
    here = ext_ref[:, pl.ds(base, rows), :]
    total = 0.5 * here
    for slot, (kind, by) in enumerate(terms):
        weight = weight_ref[slot, x_local]
        if kind == "x":
            moved = ext_ref[:, pl.ds(base + by * rows, rows), :]
        elif kind == "y":
            moved = ext_ref[:, pl.ds(base + by, rows), :]
        else:
            moved = pltpu.roll(here, (-by) % lanes, 2)
        total = total + weight[None] * moved
    return total


def load_extended(own_ref, below_ref, above_ref, ext_ref, sem, first, rows):
    count = ext_ref.shape[0]
    edge = deepest * rows
    planes_rows = own_ref.shape[1]
    copies = [
        pltpu.make_async_copy(own_ref.at[pl.ds(first, count)], ext_ref.at[:, pl.ds(edge, planes_rows)], sem.at[0]),
        pltpu.make_async_copy(below_ref, ext_ref.at[:, pl.ds(0, edge)], sem.at[1]),
        pltpu.make_async_copy(above_ref, ext_ref.at[:, pl.ds(edge + planes_rows, edge)], sem.at[2]),
    ]
    for copy in copies:
        copy.start()
    for copy in copies:
        copy.wait()


def first_filter_kernel(first, terms, rows, lanes, block, weight_ref, own_ref, below_ref, above_ref,
                        out_ref, low_ref, high_ref, ext_ref, sem):
    step = pl.program_id(0)
    planes = own_ref.shape[1] // rows

    @pl.when(step == 0)
    def _():
        load_extended(own_ref, below_ref, above_ref, ext_ref, sem, first, rows)

    def plane(i, _):
        x = step * block + i
        total = filter_plane(ext_ref, weight_ref, i, x, terms, rows, lanes)
        out_ref[:, i] = total

        @pl.when(x < deepest)
        def _():
            low_ref[:, jnp.minimum(x, deepest - 1)] = total

        @pl.when(x >= planes - deepest)
        def _():
            high_ref[:, jnp.maximum(x - (planes - deepest), 0)] = total

        return 0

    lax.fori_loop(0, block, plane, 0)


def second_filter_kernel(terms, rows, lanes, block, vec_ref, weight_ref, own_ref, below_ref, above_ref,
                         theirs_ref, mine_ref, ext_ref, sem):
    step = pl.program_id(0)
    steps = pl.num_programs(0)

    @pl.when(step == 0)
    def _():
        load_extended(own_ref, below_ref, above_ref, ext_ref, sem, 0, rows)

    start = lax.rem(step + (1 - vec_ref[0]) * (steps // 2), steps) * block

    def run(target_ref):
        def plane(i, _):
            target_ref[:, i] = filter_plane(ext_ref, weight_ref, i, start + i, terms, rows, lanes)
            return 0

        lax.fori_loop(0, block, plane, 0)

    @pl.when(step < steps // 2)
    def _():
        run(theirs_ref)

    @pl.when(step >= steps // 2)
    def _():
        run(mine_ref)


def gram_kernel(vec_ref, own_x_ref, other_x_ref, *refs):
    own_y, other_y, (out_ref, acc_ref) = refs[:2], refs[2:4], refs[4:]
    cols = own_x_ref.shape[0]
    tiles = own_x_ref.shape[1]
    group = chunk
    vec = vec_ref[0]

    def field(kind, number):
        if kind == "x":
            ref = own_x_ref if number < 2 else other_x_ref
            return ref, (number % 2) * group
        return (own_y + other_y)[number], 0

    def load(kind, number, t):
        ref, first = field(kind, number)
        return [ref[first + k, t] for k in range(group)]

    def block_of_pairs(slot, left_kind, left, right_kind, right):
        same = left % 4 == right % 4
        pairs = [(i, j) for i in range(group) for j in range(group) if not (same and j < i)]

        def step(t, accs):
            a = load(left_kind, left, t)
            b = a if same and left_kind == right_kind else load(right_kind, right, t)
            return tuple(acc + a[i] * b[j] for (i, j), acc in zip(pairs, accs))

        zero = tuple(jnp.zeros((8, 128), f32) for _ in pairs)
        accs = lax.fori_loop(0, tiles, step, zero, unroll=4)
        for (i, j), acc in zip(pairs, accs):
            row = jnp.sum(acc, axis=0, keepdims=True)
            gi = lax.rem(left * group + i + cols * vec, 2 * cols)
            gj = lax.rem(right * group + j + cols * vec, 2 * cols)
            acc_ref[slot, pl.ds(gi * 16 + gj, 1), :] = row
            acc_ref[slot, pl.ds(gj * 16 + gi, 1), :] = row

    for left in range(4):
        for right in range(left, 4):
            block_of_pairs(0, "x", left, "x", right)
            block_of_pairs(2, "y", left, "y", right)
            if left // 2 == right // 2:
                block_of_pairs(1, "y", left, "x", right)
            else:
                @pl.when(vec == 0)
                def _(left=left, right=right):
                    block_of_pairs(1, "y", left, "x", right)

                @pl.when(vec == 1)
                def _(left=left, right=right):
                    block_of_pairs(1, "y", right, "x", left)

    lane = lax.broadcasted_iota(jnp.int32, (256, 128), 1)
    inner = lax.rem(lax.broadcasted_iota(jnp.int32, (256, 128), 0), 16)
    total = jnp.zeros((16, 128), f32)
    for slot in range(3):
        sums = jnp.sum(acc_ref[slot], axis=1, keepdims=True)
        placed = jnp.where(lane == inner + 16 * slot, sums, 0.0)
        total = total + jnp.sum(placed.reshape(16, 16, 128), axis=1)
    out_ref[...] = total


def eliminate(square):
    n = square.shape[0]
    row = lax.broadcasted_iota(jnp.int32, (n, n), 0)
    col = lax.broadcasted_iota(jnp.int32, (n, n), 1)
    work = square
    inverse = jnp.where(row == col, 1.0, 0.0).astype(f32)
    factor = jnp.zeros((n, n), f32)
    for j in range(n):
        column = jnp.broadcast_to(work[:, j : j + 1], (n, n))
        scale = inverse_root(jnp.broadcast_to(column[j : j + 1, :], (n, n)))
        scaled = jnp.where(row >= j, column * scale, 0.0)
        factor = jnp.where(col == j, scaled, factor)
        work_row = jnp.broadcast_to(work[j : j + 1, :], (n, n)) * scale
        inverse_row = jnp.broadcast_to(inverse[j : j + 1, :], (n, n)) * scale
        work = jnp.where(row > j, work - scaled * work_row, work)
        inverse = jnp.where(row > j, inverse - scaled * inverse_row,
                            jnp.where(row == j, inverse_row, inverse))
    return factor, inverse


def times(a, b):
    return jnp.dot(a, b, precision=highest, preferred_element_type=f32)


def times_t(a, b):
    return lax.dot_general(a, b, (((1,), (1,)), ((), ())), precision=highest, preferred_element_type=f32)


def algebra_kernel(scale, gram_ref, alpha_ref, beta_ref, mix_ref):
    grams = [gram_ref[:, 16 * k : 16 * k + 16] for k in range(3)]
    _, inverse = eliminate(grams[0])
    coeffs = times_t(times(inverse, grams[1]), inverse)
    image = times_t(times(inverse, grams[2]), inverse)
    factor, second = eliminate(image - times_t(coeffs, coeffs))
    alpha_ref[...] = coeffs
    beta_ref[...] = factor
    mix_ref[0] = -scale * times(times(second, coeffs), inverse)
    mix_ref[1] = scale * times(second, inverse)


def combine_kernel(group_planes, mix_ref, xo_ref, xr_ref, *refs):
    ys, out_ref = refs[:-1], refs[-1]
    cols = xo_ref.shape[0]
    tiles = xo_ref.shape[1]
    sources = [(xo_ref, k) for k in range(cols)] + [(xr_ref, k) for k in range(cols)]
    for y in ys:
        sources += [(y, k) for k in range(y.shape[0])]
    for t0 in range(0, tiles, group_planes):
        for i in range(cols):
            acc = None
            for j, (ref, k) in enumerate(sources):
                term = mix_ref[i, j] * ref[k, pl.ds(t0, group_planes)]
                acc = term if acc is None else acc + term
            out_ref[i, pl.ds(t0, group_planes)] = acc


def sum_everywhere(value):
    bricks = lax.axis_size("brick")

    def brick_of(zl, x, y, c):
        return ((zl * 4 + x) * 4 + y) * 2 + c

    def split(i):
        return i // 32, (i // 8) % 4, (i // 2) % 4, i % 2

    def moved(i, dim, by):
        zl, x, y, c = split(i)
        if dim == "x":
            x = (x + by) % 4
        elif dim == "y":
            y = (y + by) % 4
        elif dim == "core":
            c = c ^ by
        else:
            zl = zl ^ by
        return brick_of(zl, x, y, c)

    def permute(v, dim, by):
        return lax.ppermute(v, "brick", [(i, moved(i, dim, by)) for i in range(bricks)])

    value = value + permute(value, "core", 1)
    pairs = {}
    for by in (1, 2, 3):
        table = []
        for brick in range(bricks):
            zl, x, y, c = split(brick)
            for vec in range(2):
                z = (2 * vec + zl + by) % 4
                table.append((brick * 2 + vec, brick_of(z % 2, x, y, c) * 2 + z // 2))
        pairs[by] = table
    near = [lax.ppermute(value, ("brick", "vec"), pairs[by]) for by in (1, 2, 3)]
    value = (value + near[0]) + (near[1] + near[2])
    for dim in ("y", "x"):
        near = [permute(value, dim, by) for by in (1, 2, 3)]
        value = (value + near[0]) + (near[1] + near[2])
    return value


def body(levels, start_block):
    own_cols, planes, rows, lanes = start_block.shape
    bricks = lax.axis_size("brick")
    brick = lax.axis_index("brick")
    vec = lax.axis_index("vec").astype(jnp.int32)
    voxel_total = bricks * planes * rows * lanes
    halves = planes // 2
    row_count = planes * rows
    upward = [(i, i + 1) for i in range(bricks - 1)]
    downward = [(i + 1, i) for i in range(bricks - 1)]
    swap = [(0, 1), (1, 0)]

    def up(value):
        return lax.ppermute(value, "brick", upward)

    def down(value):
        return lax.ppermute(value, "brick", downward)

    vec_scalar = vec.reshape(1)
    x_own = start_block.astype(f32)

    tail = jnp.concatenate(
        [to_weight(levels[position, planes - offset :]) for position, offset in enumerate(offsets_cube)], axis=0
    )
    halo = up(tail)
    x_above, x_below = [], []
    for first in range(0, own_cols, chunk):
        part = x_own[first : first + chunk]
        x_above.append(down(part[:, :deepest]))
        x_below.append(up(part[:, planes - deepest :]))
    x_theirs = lax.dynamic_slice_in_dim(x_own, (1 - vec) * halves, halves, 1)
    x_mine = lax.dynamic_slice_in_dim(x_own, vec * halves, halves, 1)
    x_other_mine = lax.ppermute(x_theirs, "vec", swap)
    x_other_theirs = lax.ppermute(x_mine, "vec", swap)

    inside_above = (brick < bricks - 1).astype(jnp.int32).reshape(1)
    root = pl.pallas_call(
        degree_kernel,
        out_shape=jax.ShapeDtypeStruct((planes, rows, lanes), f32),
        in_specs=[SMEM, VMEM, VMEM],
        out_specs=VMEM,
        compiler_params=params(16),
        name="degree",
    )(inside_above, levels, halo)
    root_above = down(root[:deepest])
    root_below = up(root[planes - deepest :])

    terms = terms_of(rows, lanes)
    slots = len(terms)
    weights = pl.pallas_call(
        weights_kernel,
        out_shape=jax.ShapeDtypeStruct((slots, planes, rows, lanes), f32),
        in_specs=[VMEM] * 5,
        out_specs=VMEM,
        compiler_params=params(24),
        name="weights",
    )(levels, halo, root, root_above, root_below)

    block = 8
    steps = planes // block
    ext = pltpu.VMEM((chunk, (planes + 2 * deepest) * rows, lanes), f32)

    def flat(value):
        return value.reshape(value.shape[0], -1, lanes)

    x_flat = flat(x_own)

    def first_filter(number):
        return pl.pallas_call(
            functools.partial(first_filter_kernel, number * chunk, terms, rows, lanes, block),
            grid=(steps,),
            out_shape=[
                jax.ShapeDtypeStruct((chunk, planes, rows, lanes), f32),
                jax.ShapeDtypeStruct((chunk, deepest, rows, lanes), f32),
                jax.ShapeDtypeStruct((chunk, deepest, rows, lanes), f32),
            ],
            in_specs=[pl.BlockSpec((slots, block, rows, lanes), lambda g: (0, g, 0, 0)), ANY, ANY, ANY],
            out_specs=[
                pl.BlockSpec((chunk, block, rows, lanes), lambda g: (0, g, 0, 0)),
                pl.BlockSpec((chunk, deepest, rows, lanes), lambda g: (0, 0, 0, 0)),
                pl.BlockSpec((chunk, deepest, rows, lanes), lambda g: (0, 0, 0, 0)),
            ],
            scratch_shapes=[ext, pltpu.SemaphoreType.DMA((3,))],
            compiler_params=params(24),
            name="first_filter",
        )(weights, x_flat, flat(x_below[number]), flat(x_above[number]))

    def second_filter(field, below, above):
        turn = steps // 2

        def place(g, vec_ref):
            return (0, lax.rem(g + (1 - vec_ref[0]) * turn, steps), 0, 0)

        return pl.pallas_call(
            functools.partial(second_filter_kernel, terms, rows, lanes, block),
            grid_spec=pltpu.PrefetchScalarGridSpec(
                num_scalar_prefetch=1,
                grid=(steps,),
                in_specs=[pl.BlockSpec((slots, block, rows, lanes), place), ANY, ANY, ANY],
                out_specs=[
                    pl.BlockSpec((chunk, block, rows, lanes), lambda g, v: (0, jnp.minimum(g, turn - 1), 0, 0)),
                    pl.BlockSpec((chunk, block, rows, lanes), lambda g, v: (0, jnp.maximum(g - turn, 0), 0, 0)),
                ],
                scratch_shapes=[ext, pltpu.SemaphoreType.DMA((3,))],
            ),
            out_shape=[jax.ShapeDtypeStruct((chunk, halves, rows, lanes), f32)] * 2,
            compiler_params=params(24),
            name="second_filter",
        )(vec_scalar, weights, flat(field), flat(below), flat(above))

    numbers = range(own_cols // chunk)
    fields, belows, aboves = [], [], []
    for number in numbers:
        field, low, high = first_filter(number)
        fields.append(field)
        aboves.append(down(low))
        belows.append(up(high))
    y_theirs, y_mine, y_other_mine, y_other_theirs = [], [], [], []
    for number in numbers:
        theirs, mine = second_filter(fields[number], belows[number], aboves[number])
        y_theirs.append(theirs)
        y_mine.append(mine)
        y_other_mine.append(lax.ppermute(theirs, "vec", swap))
        y_other_theirs.append(lax.ppermute(mine, "vec", [(0, 1)]))

    def tiled(value):
        return value.reshape(value.shape[0], -1, 8, lanes)

    gram = pl.pallas_call(
        gram_kernel,
        out_shape=jax.ShapeDtypeStruct((16, 128), f32),
        in_specs=[SMEM] + [VMEM] * 6,
        out_specs=VMEM,
        scratch_shapes=[pltpu.VMEM((3, 256, 128), f32)],
        compiler_params=params(16),
        name="gram",
    )(vec_scalar, tiled(x_mine), tiled(x_other_mine), *map(tiled, y_mine), *map(tiled, y_other_mine))
    gram = sum_everywhere(gram)

    small = jax.ShapeDtypeStruct((16, 16), f32)
    alpha, beta, mix = pl.pallas_call(
        functools.partial(algebra_kernel, math.sqrt(voxel_total)),
        out_shape=[small, small, jax.ShapeDtypeStruct((2, 16, 16), f32)],
        in_specs=[VMEM],
        out_specs=[VMEM] * 3,
        name="algebra",
    )(gram)
    own_rows = lax.dynamic_slice_in_dim(mix, vec * own_cols, own_cols, 1)
    mine_first = lax.dynamic_slice_in_dim(own_rows, vec * own_cols, own_cols, 2)
    other = lax.dynamic_slice_in_dim(own_rows, (1 - vec) * own_cols, own_cols, 2)
    table = jnp.concatenate([mine_first[0], other[0], mine_first[1], other[1]], axis=1)

    def combine(x_half, x_other, y_half, y_other):
        return pl.pallas_call(
            functools.partial(combine_kernel, 8),
            out_shape=jax.ShapeDtypeStruct((own_cols, halves * rows // 8, 8, lanes), f32),
            in_specs=[SMEM] + [VMEM] * 6,
            out_specs=VMEM,
            compiler_params=params(24),
            name="combine",
        )(table, tiled(x_half), tiled(x_other), *map(tiled, y_half), *map(tiled, y_other))

    done_mine = combine(x_mine, x_other_mine, y_mine, y_other_mine).reshape(own_cols, halves, rows, lanes)
    done_theirs = combine(x_theirs, x_other_theirs, y_theirs, y_other_theirs).reshape(own_cols, halves, rows, lanes)
    basis = jnp.zeros(start_block.shape, f32)
    basis = lax.dynamic_update_slice_in_dim(basis, done_mine, vec * halves, 1)
    basis = lax.dynamic_update_slice_in_dim(basis, done_theirs, (1 - vec) * halves, 1)
    return alpha[None], beta[None], basis


def solution(mesh):
    return jax.shard_map(
        body,
        mesh=mesh,
        in_specs=(P(None, "brick", None, None), P("vec", "brick", None, None)),
        out_specs=(P(), P(), P("vec", "brick", None, None)),
        check_vma=False,
    )
```

```python
import functools
import math

import jax
import jax.numpy as jnp
from jax import lax
from jax.experimental import pallas as pl
from jax.experimental.pallas import tpu as pltpu
from jax.sharding import PartitionSpec as P


offsets_cube = (1, 3, 9, 27)
deepest = 27
highest = lax.Precision.HIGHEST
chunk = 4
f32 = jnp.float32


ANY = pl.BlockSpec(memory_space=pl.ANY)
SMEM = pl.BlockSpec(memory_space=pltpu.SMEM)
VMEM = pl.BlockSpec(memory_space=pltpu.VMEM)


def params(mib):
    return pltpu.CompilerParams(vmem_limit_bytes=mib << 20)


def shift_rows(value, by):
    length = value.shape[-2]
    if abs(by) >= length:
        return jnp.zeros_like(value)
    rolled = pltpu.roll(value, (-by) % length, value.ndim - 2)
    row = lax.broadcasted_iota(jnp.int32, value.shape, value.ndim - 2) + by
    return jnp.where((row >= 0) & (row < length), rolled, 0.0)


def shift_lanes(value, by):
    length = value.shape[-1]
    if abs(by) >= length:
        return jnp.zeros_like(value)
    rolled = pltpu.roll(value, (-by) % length, value.ndim - 1)
    lane = lax.broadcasted_iota(jnp.int32, value.shape, value.ndim - 1) + by
    return jnp.where((lane >= 0) & (lane < length), rolled, 0.0)


def inverse_root(value):
    guess = lax.rsqrt(value)
    return guess * (1.5 - 0.5 * value * guess * guess)


def to_weight(level):
    return (level.astype(f32) + 0.5) / 256.0


def halo_start(position):
    return sum(offsets_cube[:position])


def tail_kernel(levels_ref, out_ref, raw_ref, sem):
    planes = levels_ref.shape[1]
    copies = []
    for position, offset in enumerate(offsets_cube):
        place = pl.ds(halo_start(position), offset)
        copies.append(
            pltpu.make_async_copy(
                levels_ref.at[position, pl.ds(planes - offset, offset)], raw_ref.at[place], sem.at[position]
            )
        )
    for copy in copies:
        copy.start()
    for copy in copies:
        copy.wait()
    out_ref[...] = to_weight(raw_ref[...])


def degree_kernel(flag_ref, levels_ref, halo_ref, root_ref):
    planes = levels_ref.shape[1]
    inside_above = flag_ref[0].astype(f32)

    def plane(x, _):
        total = jnp.ones(levels_ref.shape[2:], f32)
        for position, offset in enumerate(offsets_cube):
            weight = to_weight(levels_ref[position, x])
            total = total + jnp.where(x + offset < planes, 1.0, inside_above) * weight
            own = to_weight(levels_ref[position, jnp.maximum(x - offset, 0)])
            base = halo_start(position)
            far = halo_ref[base + jnp.minimum(x, offset - 1)]
            total = total + jnp.where(x >= offset, own, far)
            for axis, shift in ((1, shift_rows), (2, shift_lanes)):
                weight = to_weight(levels_ref[4 * axis + position, x])
                ones = shift(jnp.ones_like(weight), offset)
                total = total + ones * weight + shift(weight, -offset)
        root_ref[x] = inverse_root(total)
        return 0

    lax.fori_loop(0, planes, plane, 0, unroll=4)


def weights_kernel(levels_ref, halo_ref, root_ref, above_ref, below_ref, out_ref):
    planes = levels_ref.shape[1]

    def plane(x, _):
        root = root_ref[x]
        half = 0.5 * root
        slot = 0
        for position, offset in enumerate(offsets_cube):
            ahead = jnp.where(
                x + offset < planes,
                root_ref[jnp.minimum(x + offset, planes - 1)],
                above_ref[jnp.maximum(x + offset - planes, 0)],
            )
            out_ref[slot, x] = to_weight(levels_ref[position, x]) * half * ahead
            back = jnp.maximum(x - offset, 0)
            base = halo_start(position)
            weight = jnp.where(
                x >= offset, to_weight(levels_ref[position, back]), halo_ref[base + jnp.minimum(x, offset - 1)]
            )
            behind = jnp.where(
                x >= offset, root_ref[back], below_ref[jnp.clip(deepest + x - offset, 0, deepest - 1)]
            )
            out_ref[slot + 1, x] = weight * half * behind
            slot += 2
        for axis, shift in ((1, shift_rows), (2, shift_lanes)):
            for position, offset in enumerate(offsets_cube):
                if offset >= root.shape[axis - 1]:
                    continue
                weight = to_weight(levels_ref[4 * axis + position, x])
                forward = weight * half * shift(root, offset)
                out_ref[slot, x] = forward
                out_ref[slot + 1, x] = shift(forward, -offset)
                slot += 2
        return 0

    lax.fori_loop(0, planes, plane, 0, unroll=2)


def terms_of(rows, lanes):
    found = [("x", o * s) for o in offsets_cube for s in (1, -1)]
    found += [("y", o * s) for o in offsets_cube if o < rows for s in (1, -1)]
    found += [("z", o * s) for o in offsets_cube if o < lanes for s in (1, -1)]
    return found


def filter_plane(ext_ref, weight_ref, x_local, x_plane, terms, rows, lanes, put):
    for first in range(0, rows, 8):
        base = pl.multiple_of((x_plane + deepest) * rows + first, 8)
        here = ext_ref[:, pl.ds(base, 8), :]
        total = 0.5 * here
        for slot, (kind, by) in enumerate(terms):
            weight = weight_ref[slot, x_local, pl.ds(first, 8)]
            if kind == "x":
                moved = ext_ref[:, pl.ds(base + by * rows, 8), :]
            elif kind == "y":
                moved = ext_ref[:, pl.ds(base + by, 8), :]
            else:
                moved = pltpu.roll(here, (-by) % lanes, 2)
            total = total + weight[None] * moved
        put(first, total)


def load_extended(own_ref, below_ref, above_ref, ext_ref, first, rows):
    count = ext_ref.shape[0]
    edge = deepest * rows
    own_rows = own_ref.shape[1]
    ext_ref[:, pl.ds(0, edge)] = below_ref[...]
    ext_ref[:, pl.ds(edge, own_rows)] = own_ref[pl.ds(first, count)]
    ext_ref[:, pl.ds(edge + own_rows, edge)] = above_ref[...]


def first_filter_kernel(first, terms, rows, lanes, weight_ref, own_ref, below_ref, above_ref,
                        out_ref, low_ref, high_ref, ext_ref):
    planes = weight_ref.shape[1]
    load_extended(own_ref, below_ref, above_ref, ext_ref, first, rows)

    def plane(x, _):
        def put(row, total):
            out_ref[:, x, pl.ds(row, 8)] = total

        filter_plane(ext_ref, weight_ref, x, x, terms, rows, lanes, put)
        return 0

    lax.fori_loop(0, planes, plane, 0, unroll=4)
    low_ref[...] = out_ref[:, :deepest]
    high_ref[...] = out_ref[:, planes - deepest :]


def second_filter_kernel(terms, rows, lanes, vec_ref, weight_ref, own_ref, below_ref, above_ref,
                         theirs_ref, mine_ref, ext_ref):
    halves = theirs_ref.shape[1]
    load_extended(own_ref, below_ref, above_ref, ext_ref, 0, rows)
    for target_ref, start in ((theirs_ref, (1 - vec_ref[0]) * halves), (mine_ref, vec_ref[0] * halves)):

        def plane(i, _, target_ref=target_ref, start=start):
            def put(row, total):
                target_ref[:, i, pl.ds(row, 8)] = total

            filter_plane(ext_ref, weight_ref, start + i, start + i, terms, rows, lanes, put)
            return 0

        lax.fori_loop(0, halves, plane, 0, unroll=4)


def gram_kernel(early, vec_ref, own_x_ref, other_x_ref, *refs):
    if early:
        ys, (out_ref, late_ref, acc_ref) = refs[:2], refs[2:]
        for place, ref in enumerate(ys):
            late_ref[pl.ds(place * chunk, chunk)] = ref[...]
    else:
        ys, (before_ref, out_ref, acc_ref) = refs[:4], refs[4:]
    cols = own_x_ref.shape[0]
    tiles = own_x_ref.shape[1] // 2
    group = chunk
    vec = vec_ref[0]
    acc_ref[...] = jnp.zeros_like(acc_ref)

    def load(kind, number, t):
        if kind == "x":
            ref = own_x_ref if number < 2 else other_x_ref
            return [ref[(number % 2) * group + k, vec * tiles + t] for k in range(group)]
        return [ys[number][k, t] for k in range(group)]

    def block_of_pairs(slot, left_kind, left, right_kind, right):
        same = left == right
        pairs = [(i, j) for i in range(group) for j in range(group) if not (same and j < i)]

        def step(t, accs):
            a = load(left_kind, left, t)
            b = a if same and left_kind == right_kind else load(right_kind, right, t)
            return tuple(acc + a[i] * b[j] for (i, j), acc in zip(pairs, accs))

        zero = tuple(jnp.zeros((8, 128), f32) for _ in pairs)
        accs = lax.fori_loop(0, tiles, step, zero, unroll=4)
        for (i, j), acc in zip(pairs, accs):
            row = jnp.sum(acc, axis=0, keepdims=True)
            gi = lax.rem(left * group + i + cols * vec, 2 * cols)
            gj = lax.rem(right * group + j + cols * vec, 2 * cols)
            acc_ref[slot, pl.ds(gi * 16 + gj, 1), :] = row
            acc_ref[slot, pl.ds(gj * 16 + gi, 1), :] = row

    for left in range(4):
        for right in range(left, 4):
            if early:
                block_of_pairs(0, "x", left, "x", right)
            if (right < 2) == early:
                block_of_pairs(2, "y", left, "y", right)
                if left // 2 == right // 2:
                    block_of_pairs(1, "y", left, "x", right)
            if left // 2 != right // 2:
                if early:

                    @pl.when(vec == 0)
                    def _(left=left, right=right):
                        block_of_pairs(1, "y", left, "x", right)

                else:

                    @pl.when(vec == 1)
                    def _(left=left, right=right):
                        block_of_pairs(1, "y", right, "x", left)

    lane = lax.broadcasted_iota(jnp.int32, (256, 128), 1)
    inner = lax.rem(lax.broadcasted_iota(jnp.int32, (256, 128), 0), 16)
    total = jnp.zeros((16, 128), f32) if early else before_ref[...]
    for slot in range(0 if early else 1, 3):
        sums = jnp.sum(acc_ref[slot], axis=1, keepdims=True)
        placed = jnp.where(lane == inner + 16 * slot, sums, 0.0)
        total = total + jnp.sum(placed.reshape(16, 16, 128), axis=1)
    out_ref[...] = total


def eliminate(square):
    n = square.shape[0]
    row = lax.broadcasted_iota(jnp.int32, (n, n), 0)
    col = lax.broadcasted_iota(jnp.int32, (n, n), 1)
    work = square
    inverse = jnp.where(row == col, 1.0, 0.0).astype(f32)
    columns = jnp.zeros((n, n), f32)
    pivots = jnp.zeros((n, n), f32)
    across = jnp.zeros((n, n), f32)
    for j in range(n):
        column = jnp.broadcast_to(work[:, j : j + 1], (n, n))
        pivot = jnp.broadcast_to(column[j : j + 1, :], (n, n))
        factor = jnp.where(row > j, column, 0.0) / pivot
        columns = jnp.where((col == j) & (row >= j), column, columns)
        pivots = jnp.where(row == j, pivot, pivots)
        across = jnp.where(col == j, pivot, across)
        inverse = inverse - factor * jnp.broadcast_to(inverse[j : j + 1, :], (n, n))
        work = work - factor * jnp.broadcast_to(work[j : j + 1, :], (n, n))
    return columns * inverse_root(across), inverse * inverse_root(pivots)


def times(a, b):
    return jnp.dot(a, b, precision=highest, preferred_element_type=f32)


def times_t(a, b):
    return lax.dot_general(a, b, (((1,), (1,)), ((), ())), precision=highest, preferred_element_type=f32)


def algebra_kernel(scale, vec_ref, gram_ref, alpha_ref, beta_ref, table_ref):
    grams = [gram_ref[:, 16 * k : 16 * k + 16] for k in range(3)]
    _, inverse = eliminate(grams[0])
    coeffs = times_t(times(inverse, grams[1]), inverse)
    image = times_t(times(inverse, grams[2]), inverse)
    factor, second = eliminate(image - times_t(coeffs, coeffs))
    alpha_ref[...] = coeffs
    beta_ref[...] = factor
    of_image = scale * times(second, inverse)
    of_start = -scale * times(times(second, coeffs), inverse)
    first = vec_ref[0] == 0
    for place, mix in ((0, of_start), (16, of_image)):
        mine = jnp.where(first, mix[:8], mix[8:])
        table_ref[:, place : place + 8] = jnp.where(first, mine[:, :8], mine[:, 8:])
        table_ref[:, place + 8 : place + 16] = jnp.where(first, mine[:, 8:], mine[:, :8])


def combine_kernel(vec_ref, table_ref, own_x_ref, other_x_ref, *refs):
    fields = [own_x_ref, other_x_ref]
    for ref in refs:
        if sum(field.shape[0] for field in fields) < table_ref.shape[1]:
            fields.append(ref)
    out_ref = refs[-1]
    sources = [(ref, k) for ref in fields for k in range(ref.shape[0])]
    for i in range(out_ref.shape[0]):
        acc = None
        for j, (ref, k) in enumerate(sources):
            term = table_ref[i, j] * ref[k]
            acc = term if acc is None else acc + term
        out_ref[i] = acc


def brick_of(zl, x, y, c):
    return ((zl * 4 + x) * 4 + y) * 2 + c


def places():
    for zl in range(2):
        for x in range(4):
            for y in range(4):
                for c in range(2):
                    yield brick_of(zl, x, y, c), zl, x, y, c


def crowded(zl, x, y):
    return (zl, x, y) in ((0, 0, 0), (1, 3, 3))


def swap_tables(half):
    direct, first, second = [], [], []
    detour = {0: (1, 3), 1: (2, 0)}
    for brick, zl, x, y, c in places():
        for vec in range(2):
            here, there = brick * 2 + vec, brick * 2 + 1 - vec
            if not crowded(zl, x, y):
                direct.append((here, there))
                continue
            relay = brick_of(zl, (x + detour[c][half]) % 4, y, c) * 2 + 1 - vec
            first.append((here, relay))
            second.append((relay, there))
    return direct, first, second


def sum_everywhere(value):
    def moved(place, dim, by):
        _, zl, x, y, c = place
        if dim == "x":
            x = (x + by) % 4
        elif dim == "y":
            y = (y + by) % 4
        else:
            c = c ^ by
        return brick_of(zl, x, y, c)

    def permute(v, dim, by):
        return lax.ppermute(v, "brick", [(place[0], moved(place, dim, by)) for place in places()])

    value = value + permute(value, "core", 1)
    pairs = {}
    for by in (1, 2, 3):
        table = []
        for brick, zl, x, y, c in places():
            for vec in range(2):
                z = (2 * vec + zl + by) % 4
                table.append((brick * 2 + vec, brick_of(z % 2, x, y, c) * 2 + z // 2))
        pairs[by] = table
    near = [lax.ppermute(value, ("brick", "vec"), pairs[by]) for by in (1, 2, 3)]
    value = (value + near[0]) + (near[1] + near[2])
    for dim in ("y", "x"):
        near = [permute(value, dim, by) for by in (1, 2, 3)]
        value = (value + near[0]) + (near[1] + near[2])
    return value


def steps_of(levels, start_block):
    own_cols, planes, rows, lanes = start_block.shape
    bricks = lax.axis_size("brick")
    brick = lax.axis_index("brick")
    vec = lax.axis_index("vec").astype(jnp.int32)
    voxel_total = bricks * planes * rows * lanes
    halves = planes // 2
    upward = [(i, i + 1) for i in range(bricks - 1)]
    downward = [(i + 1, i) for i in range(bricks - 1)]
    swap = [(0, 1), (1, 0)]

    def up(value):
        return lax.ppermute(value, "brick", upward)

    def down(value):
        return lax.ppermute(value, "brick", downward)

    vec_scalar = vec.reshape(1)
    tail = pl.pallas_call(
        tail_kernel,
        out_shape=jax.ShapeDtypeStruct((sum(offsets_cube), rows, lanes), f32),
        in_specs=[ANY],
        out_specs=VMEM,
        scratch_shapes=[
            pltpu.VMEM((sum(offsets_cube), rows, lanes), jnp.int32),
            pltpu.SemaphoreType.DMA((len(offsets_cube),)),
        ],
        compiler_params=params(4),
        name="tail",
    )(levels)
    halo = up(tail)
    x_own = start_block.astype(f32)
    x_above, x_below = [], []
    numbers = range(own_cols // chunk)
    for number in numbers:
        part = start_block[number * chunk : (number + 1) * chunk]
        x_above.append(down(part[:, :deepest].astype(f32)))
        x_below.append(up(part[:, planes - deepest :].astype(f32)))
    both = ("brick", "vec")
    x_relayed = []
    for half in range(2):
        direct, first_pairs, second_pairs = swap_tables(half)
        part = start_block[half * chunk : (half + 1) * chunk].astype(f32)
        part = lax.ppermute(part, both, first_pairs)
        x_relayed.append(lax.ppermute(part, both, second_pairs))
    x_other = lax.ppermute(x_own, both, direct)
    x_other = x_other + jnp.concatenate(x_relayed, axis=0)

    inside_above = (brick < bricks - 1).astype(jnp.int32).reshape(1)
    root = pl.pallas_call(
        degree_kernel,
        out_shape=jax.ShapeDtypeStruct((planes, rows, lanes), f32),
        in_specs=[SMEM, VMEM, VMEM],
        out_specs=VMEM,
        compiler_params=params(4),
        name="degree",
    )(inside_above, levels, halo)
    root_above = down(root[:deepest])
    root_below = up(root[planes - deepest :])

    terms = terms_of(rows, lanes)
    slots = len(terms)
    weights = pl.pallas_call(
        weights_kernel,
        out_shape=jax.ShapeDtypeStruct((slots, planes, rows, lanes), f32),
        in_specs=[VMEM] * 5,
        out_specs=VMEM,
        compiler_params=params(4),
        name="weights",
    )(levels, halo, root, root_above, root_below)
    ext = pltpu.VMEM((chunk, (planes + 2 * deepest) * rows, lanes), f32)

    def flat(value):
        return value.reshape(value.shape[0], -1, lanes)

    x_flat = flat(x_own)

    def first_filter(number):
        edge = jax.ShapeDtypeStruct((chunk, deepest, rows, lanes), f32)
        return pl.pallas_call(
            functools.partial(first_filter_kernel, number * chunk, terms, rows, lanes),
            out_shape=[jax.ShapeDtypeStruct((chunk, planes, rows, lanes), f32), edge, edge],
            in_specs=[VMEM] * 4,
            out_specs=[VMEM] * 3,
            scratch_shapes=[ext],
            compiler_params=params(10),
        )(weights, x_flat, flat(x_below[number]), flat(x_above[number]))

    def second_filter(field, below, above):
        return pl.pallas_call(
            functools.partial(second_filter_kernel, terms, rows, lanes),
            out_shape=[jax.ShapeDtypeStruct((chunk, halves, rows, lanes), f32)] * 2,
            in_specs=[SMEM] + [VMEM] * 4,
            out_specs=[VMEM] * 2,
            scratch_shapes=[ext],
            compiler_params=params(10),
        )(vec_scalar, weights, flat(field), flat(below), flat(above))

    fields, belows, aboves = [], [], []
    for number in numbers:
        field, low, high = first_filter(number)
        fields.append(field)
        aboves.append(down(low))
        belows.append(up(high))
    y_theirs, y_mine, y_other_mine = [], [], []
    for number in numbers:
        theirs, mine = second_filter(fields[number], belows[number], aboves[number])
        y_theirs.append(theirs)
        y_mine.append(mine)
        y_other_mine.append(lax.ppermute(theirs, "vec", swap))

    def tiled(value):
        return value.reshape(value.shape[0], -1, 8, lanes) if value.shape[2] != 8 else value

    def gram_call(early, *operands):
        out = jax.ShapeDtypeStruct((2 * own_cols, 128), f32)
        late = jax.ShapeDtypeStruct((own_cols, halves * rows // 8, 8, lanes), f32)
        return pl.pallas_call(
            functools.partial(gram_kernel, early),
            out_shape=(out, late) if early else out,
            in_specs=[SMEM] + [VMEM] * len(operands),
            out_specs=(VMEM, VMEM) if early else VMEM,
            scratch_shapes=[pltpu.VMEM((3, 256, 128), f32)],
            compiler_params=params(4),
            name="gram_early" if early else "gram_late",
        )(vec_scalar, *operands)

    mine_tiled = [tiled(value) for value in (x_own, x_other, *y_mine)]
    partial_gram, outgoing = gram_call(True, *mine_tiled)
    late = lax.ppermute(outgoing, "vec", [(0, 1)])
    gram = gram_call(False, *mine_tiled, *map(tiled, y_other_mine), partial_gram)
    gram = sum_everywhere(gram)

    small = jax.ShapeDtypeStruct((16, 16), f32)
    alpha, beta, table = pl.pallas_call(
        functools.partial(algebra_kernel, math.sqrt(voxel_total)),
        out_shape=[small, small, jax.ShapeDtypeStruct((own_cols, 4 * own_cols), f32)],
        in_specs=[SMEM, VMEM],
        out_specs=[VMEM] * 3,
        compiler_params=params(4),
        name="algebra",
    )(vec_scalar, gram)

    def combine(mine, *fields, before=None):
        parts = 4
        block_tiles = halves * rows // 8 // parts

        def whole(g, vec_ref):
            half = vec_ref[0] if mine else 1 - vec_ref[0]
            return (0, half * parts + g, 0, 0)

        extra = [] if before is None else [before]
        specs = [pl.BlockSpec((own_cols, block_tiles, 8, lanes), whole)] * 2
        for value in fields[2:]:
            specs.append(pl.BlockSpec((value.shape[0], block_tiles, 8, lanes), lambda g, vec_ref: (0, g, 0, 0)))
        return pl.pallas_call(
            combine_kernel,
            grid_spec=pltpu.PrefetchScalarGridSpec(
                num_scalar_prefetch=1,
                grid=(parts,),
                in_specs=[SMEM] + specs + [ANY] * len(extra),
                out_specs=pl.BlockSpec((own_cols, block_tiles, 8, lanes), whole),
            ),
            out_shape=jax.ShapeDtypeStruct((own_cols, planes * rows // 8, 8, lanes), f32),
            input_output_aliases={2 + len(fields): 0} if extra else {},
            compiler_params=params(10),
            name="combine",
        )(vec_scalar, table, *map(tiled, fields), *extra)

    basis = combine(True, x_own, x_other, *y_mine, *y_other_mine)
    basis = combine(False, x_own, x_other, *y_theirs, late, before=basis)
    return alpha[None], beta[None], basis.reshape(start_block.shape)


def solution(mesh):
    return jax.shard_map(
        steps_of,
        mesh=mesh,
        in_specs=(P(None, "brick", None, None), P("vec", "brick", None, None)),
        out_specs=(P(), P(), P("vec", "brick", None, None)),
        check_vma=False,
    )
```

```python
import functools
import math

import jax
import jax.numpy as jnp
from jax import lax
from jax.experimental import pallas as pl
from jax.experimental.pallas import tpu as pltpu
from jax.sharding import PartitionSpec as P


offsets_cube = (1, 3, 9, 27)
deepest = 27
highest = lax.Precision.HIGHEST
chunk = 4
f32 = jnp.float32


ANY = pl.BlockSpec(memory_space=pl.ANY)
SMEM = pl.BlockSpec(memory_space=pltpu.SMEM)
VMEM = pl.BlockSpec(memory_space=pltpu.VMEM)
HBM = pl.BlockSpec(memory_space=pltpu.HBM)


def params(mib):
    return pltpu.CompilerParams(vmem_limit_bytes=mib << 20)


def shift_rows(value, by):
    length = value.shape[-2]
    if abs(by) >= length:
        return jnp.zeros_like(value)
    rolled = pltpu.roll(value, (-by) % length, value.ndim - 2)
    row = lax.broadcasted_iota(jnp.int32, value.shape, value.ndim - 2) + by
    return jnp.where((row >= 0) & (row < length), rolled, 0.0)


def shift_lanes(value, by):
    length = value.shape[-1]
    if abs(by) >= length:
        return jnp.zeros_like(value)
    rolled = pltpu.roll(value, (-by) % length, value.ndim - 1)
    lane = lax.broadcasted_iota(jnp.int32, value.shape, value.ndim - 1) + by
    return jnp.where((lane >= 0) & (lane < length), rolled, 0.0)


def inverse_root(value):
    guess = lax.rsqrt(value)
    return guess * (1.5 - 0.5 * value * guess * guess)


def to_weight(level):
    return (level.astype(f32) + 0.5) / 256.0


def halo_start(position):
    return sum(offsets_cube[:position])


def tail_kernel(levels_ref, out_ref, raw_ref, sem):
    planes = levels_ref.shape[1]
    copies = []
    for position, offset in enumerate(offsets_cube):
        place = pl.ds(halo_start(position), offset)
        copies.append(
            pltpu.make_async_copy(
                levels_ref.at[position, pl.ds(planes - offset, offset)], raw_ref.at[place], sem.at[position]
            )
        )
    for copy in copies:
        copy.start()
    for copy in copies:
        copy.wait()
    out_ref[...] = to_weight(raw_ref[...])


def degree_kernel(levels_ref, halo_ref, start_ref, root_ref, *edge_refs):
    planes = levels_ref.shape[1]
    inside_above = (lax.axis_index("brick") < lax.axis_size("brick") - 1).astype(f32)

    def plane(x, _):
        total = jnp.ones(levels_ref.shape[2:], f32)
        for position, offset in enumerate(offsets_cube):
            weight = to_weight(levels_ref[position, x])
            total = total + jnp.where(x + offset < planes, 1.0, inside_above) * weight
            own = to_weight(levels_ref[position, jnp.maximum(x - offset, 0)])
            base = halo_start(position)
            far = halo_ref[base + jnp.minimum(x, offset - 1)]
            total = total + jnp.where(x >= offset, own, far)
            for axis, shift in ((1, shift_rows), (2, shift_lanes)):
                weight = to_weight(levels_ref[4 * axis + position, x])
                ones = shift(jnp.ones_like(weight), offset)
                total = total + ones * weight + shift(weight, -offset)
        root_ref[x] = inverse_root(total)
        return 0

    lax.fori_loop(0, planes, plane, 0, unroll=4)
    for number in range(len(edge_refs) // 2):
        low_ref, high_ref = edge_refs[2 * number : 2 * number + 2]

        def edge(x, _, number=number, low_ref=low_ref, high_ref=high_ref):
            for ref, far in ((low_ref, x), (high_ref, x + planes - deepest)):
                ref[:, x] = start_ref[pl.ds(number * chunk, chunk), far] * root_ref[far][None]
            return 0

        lax.fori_loop(0, deepest, edge, 0, unroll=3)


def weights_kernel(levels_ref, halo_ref, out_ref):
    planes = levels_ref.shape[1]

    def plane(x, _):
        slot = 0
        for position, offset in enumerate(offsets_cube):
            out_ref[slot, x] = to_weight(levels_ref[position, x])
            own = to_weight(levels_ref[position, jnp.maximum(x - offset, 0)])
            far = halo_ref[halo_start(position) + jnp.minimum(x, offset - 1)]
            out_ref[slot + 1, x] = jnp.where(x >= offset, own, far)
            slot += 2
        for axis, shift in ((1, shift_rows), (2, shift_lanes)):
            for position, offset in enumerate(offsets_cube):
                if offset >= levels_ref.shape[axis + 1]:
                    continue
                weight = to_weight(levels_ref[4 * axis + position, x])
                forward = weight * shift(jnp.ones_like(weight), offset)
                out_ref[slot, x] = forward
                out_ref[slot + 1, x] = shift(forward, -offset)
                slot += 2
        return 0

    lax.fori_loop(0, planes, plane, 0, unroll=2)


def terms_of(rows, lanes):
    found = [("x", o * s) for o in offsets_cube for s in (1, -1)]
    found += [("y", o * s) for o in offsets_cube if o < rows for s in (1, -1)]
    found += [("z", o * s) for o in offsets_cube if o < lanes for s in (1, -1)]
    return found


def filter_plane(ext_ref, weight_ref, root_ref, own_ref, first, x, terms, rows, lanes, put):
    for row in range(0, rows, 8):
        base = pl.multiple_of((x + deepest) * rows + row, 8)
        here = ext_ref[:, pl.ds(base, 8), :]
        total = None
        for slot, (kind, by) in enumerate(terms):
            weight = weight_ref[slot, x, pl.ds(row, 8)]
            if kind == "x":
                moved = ext_ref[:, pl.ds(base + by * rows, 8), :]
            elif kind == "y":
                moved = ext_ref[:, pl.ds(base + by, 8), :]
            else:
                moved = pltpu.roll(here, (-by) % lanes, 2)
            term = weight[None] * moved
            total = term if total is None else total + term
        own = own_ref[pl.ds(first, ext_ref.shape[0]), x, pl.ds(row, 8)]
        put(row, 0.5 * (own + root_ref[x, pl.ds(row, 8)][None] * total))


def load_extended(own_ref, below_ref, above_ref, root_ref, ext_ref, first, rows):
    count = ext_ref.shape[0]
    planes = root_ref.shape[0]
    edge = deepest * rows
    ext_ref[:, pl.ds(0, edge)] = below_ref[...]
    ext_ref[:, pl.ds(edge + planes * rows, edge)] = above_ref[...]

    def plane(x, _):
        place = pl.ds(pl.multiple_of(edge + x * rows, rows), rows)
        ext_ref[:, place] = own_ref[pl.ds(first, count), x] * root_ref[x][None]
        return 0

    lax.fori_loop(0, planes, plane, 0, unroll=4)


def first_filter_kernel(first, terms, rows, lanes, weight_ref, root_ref, own_ref, below_ref, above_ref,
                        out_ref, low_ref, high_ref, *rest):
    ext_ref = rest[-1]
    planes = weight_ref.shape[1]
    load_extended(own_ref, below_ref, above_ref, root_ref, ext_ref, first, rows)

    def plane(x, _):
        def put(row, total):
            out_ref[:, x, pl.ds(row, 8)] = total

        filter_plane(ext_ref, weight_ref, root_ref, own_ref, first, x, terms, rows, lanes, put)
        return 0

    lax.fori_loop(0, planes, plane, 0, unroll=4)
    low_ref[...] = out_ref[:, :deepest] * root_ref[:deepest][None]
    high_ref[...] = out_ref[:, planes - deepest :] * root_ref[planes - deepest :][None]


def second_filter_kernel(theirs, terms, rows, lanes, weight_ref, root_ref, own_ref, below_ref, above_ref,
                         out_ref, *rest):
    ext_ref = rest[-1]
    halves = out_ref.shape[1]
    load_extended(own_ref, below_ref, above_ref, root_ref, ext_ref, 0, rows)
    vec = lax.axis_index("vec")
    start = (1 - vec if theirs else vec) * halves

    def plane(i, _):
        def put(row, total):
            out_ref[:, i, pl.ds(row, 8)] = total

        filter_plane(ext_ref, weight_ref, root_ref, own_ref, 0, start + i, terms, rows, lanes, put)
        return 0

    lax.fori_loop(0, halves, plane, 0, unroll=4)


def gram_kernel(early, own_x_ref, other_x_ref, *refs):
    if early:
        ys, (out_ref, late_ref, acc_ref) = refs[:2], refs[2:]
        for place, ref in enumerate(ys):
            late_ref[pl.ds(place * chunk, chunk)] = ref[...]
    else:
        ys, (before_ref, out_ref, acc_ref) = refs[:4], refs[4:]
    cols = own_x_ref.shape[0]
    tiles = own_x_ref.shape[1] // 2
    group = chunk
    vec = lax.axis_index("vec")
    acc_ref[...] = jnp.zeros_like(acc_ref)

    def load(kind, number, t):
        if kind == "x":
            ref = own_x_ref if number < 2 else other_x_ref
            return [ref[(number % 2) * group + k, vec * tiles + t] for k in range(group)]
        return [ys[number][k, t] for k in range(group)]

    def block_of_pairs(slot, left_kind, left, right_kind, right):
        same = left == right
        pairs = [(i, j) for i in range(group) for j in range(group) if not (same and j < i)]

        def step(t, accs):
            a = load(left_kind, left, t)
            b = a if same and left_kind == right_kind else load(right_kind, right, t)
            return tuple(acc + a[i] * b[j] for (i, j), acc in zip(pairs, accs))

        zero = tuple(jnp.zeros((8, 128), f32) for _ in pairs)
        accs = lax.fori_loop(0, tiles, step, zero, unroll=4)
        for (i, j), acc in zip(pairs, accs):
            row = jnp.sum(acc, axis=0, keepdims=True)
            gi = lax.rem(left * group + i + cols * vec, 2 * cols)
            gj = lax.rem(right * group + j + cols * vec, 2 * cols)
            acc_ref[slot, pl.ds(gi * 16 + gj, 1), :] = row
            acc_ref[slot, pl.ds(gj * 16 + gi, 1), :] = row

    for left in range(4):
        for right in range(left, 4):
            if early:
                block_of_pairs(0, "x", left, "x", right)
            if (right < 2) == early:
                block_of_pairs(2, "y", left, "y", right)
                if left // 2 == right // 2:
                    block_of_pairs(1, "y", left, "x", right)
            if left // 2 != right // 2:
                if early:

                    @pl.when(vec == 0)
                    def _(left=left, right=right):
                        block_of_pairs(1, "y", left, "x", right)

                else:

                    @pl.when(vec == 1)
                    def _(left=left, right=right):
                        block_of_pairs(1, "y", right, "x", left)

    lane = lax.broadcasted_iota(jnp.int32, (256, 128), 1)
    inner = lax.rem(lax.broadcasted_iota(jnp.int32, (256, 128), 0), 16)
    total = jnp.zeros((16, 128), f32) if early else before_ref[...]
    for slot in range(0 if early else 1, 3):
        sums = jnp.sum(acc_ref[slot], axis=1, keepdims=True)
        placed = jnp.where(lane == inner + 16 * slot, sums, 0.0)
        total = total + jnp.sum(placed.reshape(16, 16, 128), axis=1)
    out_ref[...] = total


def eliminate(square):
    n = square.shape[0]
    row = lax.broadcasted_iota(jnp.int32, (n, n), 0)
    col = lax.broadcasted_iota(jnp.int32, (n, n), 1)
    work = square
    inverse = jnp.where(row == col, 1.0, 0.0).astype(f32)
    columns = jnp.zeros((n, n), f32)
    pivots = jnp.zeros((n, n), f32)
    across = jnp.zeros((n, n), f32)
    for j in range(n):
        column = jnp.broadcast_to(work[:, j : j + 1], (n, n))
        pivot = jnp.broadcast_to(column[j : j + 1, :], (n, n))
        factor = jnp.where(row > j, column, 0.0) / pivot
        columns = jnp.where((col == j) & (row >= j), column, columns)
        pivots = jnp.where(row == j, pivot, pivots)
        across = jnp.where(col == j, pivot, across)
        inverse = inverse - factor * jnp.broadcast_to(inverse[j : j + 1, :], (n, n))
        work = work - factor * jnp.broadcast_to(work[j : j + 1, :], (n, n))
    return columns * inverse_root(across), inverse * inverse_root(pivots)


def times(a, b):
    return jnp.dot(a, b, precision=highest, preferred_element_type=f32)


def times_t(a, b):
    return lax.dot_general(a, b, (((1,), (1,)), ((), ())), precision=highest, preferred_element_type=f32)


def algebra_kernel(scale, gram_ref, alpha_ref, beta_ref, table_ref, vec_ref):
    grams = [gram_ref[:, 16 * k : 16 * k + 16] for k in range(3)]
    _, inverse = eliminate(grams[0])
    coeffs = times_t(times(inverse, grams[1]), inverse)
    image = times_t(times(inverse, grams[2]), inverse)
    factor, second = eliminate(image - times_t(coeffs, coeffs))
    alpha_ref[...] = coeffs
    beta_ref[...] = factor
    of_image = scale * times(second, inverse)
    of_start = -scale * times(times(second, coeffs), inverse)
    vec = lax.axis_index("vec").astype(jnp.int32)
    vec_ref[0] = vec
    first = vec == 0
    for place, mix in ((0, of_start), (16, of_image)):
        mine = jnp.where(first, mix[:8], mix[8:])
        table_ref[:, place : place + 8] = jnp.where(first, mine[:, :8], mine[:, 8:])
        table_ref[:, place + 8 : place + 16] = jnp.where(first, mine[:, 8:], mine[:, :8])


def combine_kernel(vec_ref, table_ref, own_x_ref, other_x_ref, *refs):
    fields = [own_x_ref, other_x_ref]
    for ref in refs:
        if sum(field.shape[0] for field in fields) < table_ref.shape[1]:
            fields.append(ref)
    out_ref = refs[-1]
    sources = [(ref, k) for ref in fields for k in range(ref.shape[0])]
    for i in range(out_ref.shape[0]):
        acc = None
        for j, (ref, k) in enumerate(sources):
            term = table_ref[i, j] * ref[k]
            acc = term if acc is None else acc + term
        out_ref[i] = acc


def brick_of(zl, x, y, c):
    return ((zl * 4 + x) * 4 + y) * 2 + c


def places():
    for zl in range(2):
        for x in range(4):
            for y in range(4):
                for c in range(2):
                    yield brick_of(zl, x, y, c), zl, x, y, c


def crowded(zl, x, y):
    return (zl, x, y) in ((0, 0, 0), (1, 3, 3))


def swap_tables(half):
    direct, first, second = [], [], []
    detour = {0: (1, 3), 1: (2, 0)}
    for brick, zl, x, y, c in places():
        for vec in range(2):
            here, there = brick * 2 + vec, brick * 2 + 1 - vec
            if not crowded(zl, x, y):
                direct.append((here, there))
                continue
            relay = brick_of(zl, (x + detour[c][half]) % 4, y, c) * 2 + 1 - vec
            first.append((here, relay))
            second.append((relay, there))
    return direct, first, second


def sum_everywhere(value):
    def moved(place, dim, by):
        _, zl, x, y, c = place
        if dim == "x":
            x = (x + by) % 4
        elif dim == "y":
            y = (y + by) % 4
        else:
            c = c ^ by
        return brick_of(zl, x, y, c)

    def permute(v, dim, by):
        return lax.ppermute(v, "brick", [(place[0], moved(place, dim, by)) for place in places()])

    value = value + permute(value, "core", 1)
    pairs = {}
    for by in (1, 2, 3):
        table = []
        for brick, zl, x, y, c in places():
            for vec in range(2):
                z = (2 * vec + zl + by) % 4
                table.append((brick * 2 + vec, brick_of(z % 2, x, y, c) * 2 + z // 2))
        pairs[by] = table
    near = [lax.ppermute(value, ("brick", "vec"), pairs[by]) for by in (1, 2, 3)]
    value = (value + near[0]) + (near[1] + near[2])
    for dim in ("y", "x"):
        near = [permute(value, dim, by) for by in (1, 2, 3)]
        value = (value + near[0]) + (near[1] + near[2])
    return value


def steps_of(levels, start_block):
    own_cols, planes, rows, lanes = start_block.shape
    bricks = lax.axis_size("brick")
    voxel_total = bricks * planes * rows * lanes
    halves = planes // 2
    upward = [(i, i + 1) for i in range(bricks - 1)]
    downward = [(i + 1, i) for i in range(bricks - 1)]
    swap = [(0, 1), (1, 0)]

    def up(value):
        return lax.ppermute(value, "brick", upward)

    def down(value):
        return lax.ppermute(value, "brick", downward)

    tail = pl.pallas_call(
        tail_kernel,
        out_shape=jax.ShapeDtypeStruct((sum(offsets_cube), rows, lanes), f32),
        in_specs=[HBM],
        out_specs=VMEM,
        scratch_shapes=[
            pltpu.VMEM((sum(offsets_cube), rows, lanes), jnp.int32),
            pltpu.SemaphoreType.DMA((len(offsets_cube),)),
        ],
        compiler_params=params(60),
        name="tail",
    )(levels)
    halo = up(tail)
    x_own = start_block.astype(f32)
    both = ("brick", "vec")
    x_relayed = []
    for half in range(2):
        direct, first_pairs, second_pairs = swap_tables(half)
        part = x_own[half * chunk : (half + 1) * chunk]
        part = lax.ppermute(part, both, first_pairs)
        x_relayed.append(lax.ppermute(part, both, second_pairs))
    x_other = lax.ppermute(x_own, both, direct)
    x_other = x_other + jnp.concatenate(x_relayed, axis=0)

    numbers = range(own_cols // chunk)
    edge = jax.ShapeDtypeStruct((chunk, deepest, rows, lanes), f32)
    root, *edges = pl.pallas_call(
        degree_kernel,
        out_shape=[jax.ShapeDtypeStruct((planes, rows, lanes), f32)] + [edge] * (2 * len(numbers)),
        in_specs=[VMEM] * 3,
        out_specs=[VMEM] * (1 + 2 * len(numbers)),
        compiler_params=params(4),
        name="degree",
    )(levels, halo, x_own)
    x_above, x_below = [], []
    for number in numbers:
        x_above.append(down(edges[2 * number]))
        x_below.append(up(edges[2 * number + 1]))

    terms = terms_of(rows, lanes)
    slots = len(terms)
    weights = pl.pallas_call(
        weights_kernel,
        out_shape=jax.ShapeDtypeStruct((slots, planes, rows, lanes), f32),
        in_specs=[VMEM] * 2,
        out_specs=VMEM,
        compiler_params=params(4),
        name="weights",
    )(levels, halo)
    ext = pltpu.VMEM((chunk, (planes + 2 * deepest) * rows, lanes), f32)

    def flat(value):
        return value.reshape(value.shape[0], -1, lanes)

    keep = jax.ShapeDtypeStruct(weights.shape, f32)

    def first_filter(number, weights):
        field = jax.ShapeDtypeStruct((chunk, planes, rows, lanes), f32)
        return pl.pallas_call(
            functools.partial(first_filter_kernel, number * chunk, terms, rows, lanes),
            out_shape=[field, edge, edge, keep],
            in_specs=[VMEM] * 5,
            out_specs=[VMEM] * 4,
            scratch_shapes=[ext],
            input_output_aliases={0: 3},
            compiler_params=params(8),
        )(weights, root, x_own, flat(x_below[number]), flat(x_above[number]))

    def second_filter(theirs, number, weights):
        return pl.pallas_call(
            functools.partial(second_filter_kernel, theirs, terms, rows, lanes),
            out_shape=[jax.ShapeDtypeStruct((chunk, halves, rows, lanes), f32), keep],
            in_specs=[VMEM] * 5,
            out_specs=[VMEM] * 2,
            scratch_shapes=[ext],
            input_output_aliases={0: 1},
            compiler_params=params(8),
        )(weights, root, fields[number], flat(belows[number]), flat(aboves[number]))

    fields, belows, aboves = [], [], []
    for number in numbers:
        field, low, high, weights = first_filter(number, weights)
        fields.append(field)
        aboves.append(down(low))
        belows.append(up(high))
    y_theirs, y_mine, y_other_mine = [], [], []
    for number in numbers:
        theirs, weights = second_filter(True, number, weights)
        y_theirs.append(theirs)
        y_other_mine.append(lax.ppermute(theirs, "vec", swap))
    for number in numbers:
        mine, weights = second_filter(False, number, weights)
        y_mine.append(mine)

    def tiled(value):
        return value.reshape(value.shape[0], -1, 8, lanes) if value.shape[2] != 8 else value

    def gram_call(early, *operands):
        out = jax.ShapeDtypeStruct((2 * own_cols, 128), f32)
        late = jax.ShapeDtypeStruct((own_cols, halves * rows // 8, 8, lanes), f32)
        return pl.pallas_call(
            functools.partial(gram_kernel, early),
            out_shape=(out, late) if early else out,
            in_specs=[VMEM] * len(operands),
            out_specs=(VMEM, VMEM) if early else VMEM,
            scratch_shapes=[pltpu.VMEM((3, 256, 128), f32)],
            compiler_params=params(4),
            name="gram_early" if early else "gram_late",
        )(*operands)

    mine_tiled = [tiled(value) for value in (x_own, x_other, *y_mine)]
    partial_gram, outgoing = gram_call(True, *mine_tiled)
    late = lax.ppermute(outgoing, "vec", [(0, 1)])
    gram = gram_call(False, *mine_tiled, *map(tiled, y_other_mine), partial_gram)
    gram = sum_everywhere(gram)

    small = jax.ShapeDtypeStruct((16, 16), f32)
    alpha, beta, table, vec_scalar = pl.pallas_call(
        functools.partial(algebra_kernel, math.sqrt(voxel_total)),
        out_shape=[small, small, jax.ShapeDtypeStruct((own_cols, 4 * own_cols), f32), jax.ShapeDtypeStruct((1,), jnp.int32)],
        in_specs=[VMEM],
        out_specs=[VMEM] * 3 + [SMEM],
        compiler_params=params(4),
        name="algebra",
    )(gram)

    def combine(mine, *fields, before=None):
        parts = 4
        block_tiles = halves * rows // 8 // parts

        def whole(g, vec_ref):
            half = vec_ref[0] if mine else 1 - vec_ref[0]
            return (0, half * parts + g, 0, 0)

        extra = [] if before is None else [before]
        specs = [pl.BlockSpec((own_cols, block_tiles, 8, lanes), whole)] * 2
        for value in fields[2:]:
            specs.append(pl.BlockSpec((value.shape[0], block_tiles, 8, lanes), lambda g, vec_ref: (0, g, 0, 0)))
        return pl.pallas_call(
            combine_kernel,
            grid_spec=pltpu.PrefetchScalarGridSpec(
                num_scalar_prefetch=1,
                grid=(parts,),
                in_specs=[SMEM] + specs + [ANY] * len(extra),
                out_specs=pl.BlockSpec((own_cols, block_tiles, 8, lanes), whole),
            ),
            out_shape=jax.ShapeDtypeStruct((own_cols, planes * rows // 8, 8, lanes), f32),
            input_output_aliases={2 + len(fields): 0} if extra else {},
            compiler_params=params(8),
            name="combine",
        )(vec_scalar, table, *map(tiled, fields), *extra)

    basis = combine(True, x_own, x_other, *y_mine, *y_other_mine)
    basis = combine(False, x_own, x_other, *y_theirs, late, before=basis)
    return alpha[None], beta[None], basis.reshape(start_block.shape)


def solution(mesh):
    return jax.shard_map(
        steps_of,
        mesh=mesh,
        in_specs=(P(None, "brick", None, None), P("vec", "brick", None, None)),
        out_specs=(P(), P(), P("vec", "brick", None, None)),
        check_vma=False,
    )
```

```python
import functools
import math

import jax
import jax.numpy as jnp
from jax import lax
from jax.experimental import pallas as pl
from jax.experimental.pallas import tpu as pltpu
from jax.sharding import PartitionSpec as P


offsets_cube = (1, 3, 9, 27)
deepest = 27
highest = lax.Precision.HIGHEST
chunk = 4
f32 = jnp.float32


ANY = pl.BlockSpec(memory_space=pl.ANY)
SMEM = pl.BlockSpec(memory_space=pltpu.SMEM)
VMEM = pl.BlockSpec(memory_space=pltpu.VMEM)
HBM = pl.BlockSpec(memory_space=pltpu.HBM)


def params(mib):
    return pltpu.CompilerParams(vmem_limit_bytes=mib << 20)


def shift_rows(value, by):
    length = value.shape[-2]
    if abs(by) >= length:
        return jnp.zeros_like(value)
    rolled = pltpu.roll(value, (-by) % length, value.ndim - 2)
    row = lax.broadcasted_iota(jnp.int32, value.shape, value.ndim - 2) + by
    return jnp.where((row >= 0) & (row < length), rolled, 0.0)


def shift_lanes(value, by):
    length = value.shape[-1]
    if abs(by) >= length:
        return jnp.zeros_like(value)
    rolled = pltpu.roll(value, (-by) % length, value.ndim - 1)
    lane = lax.broadcasted_iota(jnp.int32, value.shape, value.ndim - 1) + by
    return jnp.where((lane >= 0) & (lane < length), rolled, 0.0)


def inverse_root(value):
    guess = lax.rsqrt(value)
    return guess * (1.5 - 0.5 * value * guess * guess)


def to_weight(level):
    return (level.astype(f32) + 0.5) / 256.0


def halo_start(position):
    return sum(offsets_cube[:position])


def tail_kernel(levels_ref, out_ref, raw_ref, sem):
    planes = levels_ref.shape[1]
    copies = []
    for position, offset in enumerate(offsets_cube):
        place = pl.ds(halo_start(position), offset)
        copies.append(
            pltpu.make_async_copy(
                levels_ref.at[position, pl.ds(planes - offset, offset)], raw_ref.at[place], sem.at[position]
            )
        )
    for copy in copies:
        copy.start()
    for copy in copies:
        copy.wait()
    out_ref[...] = to_weight(raw_ref[...])


def degree_kernel(levels_ref, halo_ref, start_ref, root_ref, *edge_refs):
    planes = levels_ref.shape[1]
    inside_above = (lax.axis_index("brick") < lax.axis_size("brick") - 1).astype(f32)

    def plane(x, _):
        total = jnp.ones(levels_ref.shape[2:], f32)
        for position, offset in enumerate(offsets_cube):
            weight = to_weight(levels_ref[position, x])
            total = total + jnp.where(x + offset < planes, 1.0, inside_above) * weight
            own = to_weight(levels_ref[position, jnp.maximum(x - offset, 0)])
            base = halo_start(position)
            far = halo_ref[base + jnp.minimum(x, offset - 1)]
            total = total + jnp.where(x >= offset, own, far)
            for axis, shift in ((1, shift_rows), (2, shift_lanes)):
                weight = to_weight(levels_ref[4 * axis + position, x])
                ones = shift(jnp.ones_like(weight), offset)
                total = total + ones * weight + shift(weight, -offset)
        root_ref[x] = inverse_root(total)
        return 0

    lax.fori_loop(0, planes, plane, 0, unroll=4)
    for number in range(len(edge_refs) // 2):
        low_ref, high_ref = edge_refs[2 * number : 2 * number + 2]

        def edge(x, _, number=number, low_ref=low_ref, high_ref=high_ref):
            for ref, far in ((low_ref, x), (high_ref, x + planes - deepest)):
                ref[:, x] = start_ref[pl.ds(number * chunk, chunk), far] * root_ref[far][None]
            return 0

        lax.fori_loop(0, deepest, edge, 0, unroll=3)


def weights_kernel(levels_ref, halo_ref, out_ref):
    planes = levels_ref.shape[1]

    def plane(x, _):
        slot = 0
        for position, offset in enumerate(offsets_cube):
            out_ref[slot, x] = to_weight(levels_ref[position, x])
            own = to_weight(levels_ref[position, jnp.maximum(x - offset, 0)])
            far = halo_ref[halo_start(position) + jnp.minimum(x, offset - 1)]
            out_ref[slot + 1, x] = jnp.where(x >= offset, own, far)
            slot += 2
        for axis, shift in ((1, shift_rows), (2, shift_lanes)):
            for position, offset in enumerate(offsets_cube):
                if offset >= levels_ref.shape[axis + 1]:
                    continue
                weight = to_weight(levels_ref[4 * axis + position, x])
                forward = weight * shift(jnp.ones_like(weight), offset)
                out_ref[slot, x] = forward
                out_ref[slot + 1, x] = shift(forward, -offset)
                slot += 2
        return 0

    lax.fori_loop(0, planes, plane, 0, unroll=4)


def terms_of(rows, lanes):
    found = [("x", o * s) for o in offsets_cube for s in (1, -1)]
    found += [("y", o * s) for o in offsets_cube if o < rows for s in (1, -1)]
    found += [("z", o * s) for o in offsets_cube if o < lanes for s in (1, -1)]
    return found


def filter_plane(ext_ref, weight_ref, root_ref, own_ref, first, x, terms, rows, lanes, put):
    for row in range(0, rows, 8):
        base = pl.multiple_of((x + deepest) * rows + row, 8)
        here = ext_ref[:, pl.ds(base, 8), :]
        total = None
        for slot, (kind, by) in enumerate(terms):
            weight = weight_ref[slot, x, pl.ds(row, 8)]
            if kind == "x":
                moved = ext_ref[:, pl.ds(base + by * rows, 8), :]
            elif kind == "y":
                moved = ext_ref[:, pl.ds(base + by, 8), :]
            else:
                moved = pltpu.roll(here, (-by) % lanes, 2)
            term = weight[None] * moved
            total = term if total is None else total + term
        own = own_ref[pl.ds(first, ext_ref.shape[0]), x, pl.ds(row, 8)]
        put(row, 0.5 * (own + root_ref[x, pl.ds(row, 8)][None] * total))


def load_extended(own_ref, below_ref, above_ref, root_ref, ext_ref, first, rows):
    count = ext_ref.shape[0]
    planes = root_ref.shape[0]
    edge = deepest * rows
    ext_ref[:, pl.ds(0, edge)] = below_ref[...]
    ext_ref[:, pl.ds(edge + planes * rows, edge)] = above_ref[...]

    def plane(x, _):
        place = pl.ds(pl.multiple_of(edge + x * rows, rows), rows)
        ext_ref[:, place] = own_ref[pl.ds(first, count), x] * root_ref[x][None]
        return 0

    lax.fori_loop(0, planes, plane, 0, unroll=4)


def first_filter_kernel(first, terms, rows, lanes, weight_ref, root_ref, own_ref, below_ref, above_ref,
                        out_ref, low_ref, high_ref, *rest):
    ext_ref = rest[-1]
    planes = weight_ref.shape[1]
    load_extended(own_ref, below_ref, above_ref, root_ref, ext_ref, first, rows)

    def plane(x, _):
        def put(row, total):
            out_ref[:, x, pl.ds(row, 8)] = total

        filter_plane(ext_ref, weight_ref, root_ref, own_ref, first, x, terms, rows, lanes, put)
        return 0

    lax.fori_loop(0, planes, plane, 0, unroll=4)
    low_ref[...] = out_ref[:, :deepest] * root_ref[:deepest][None]
    high_ref[...] = out_ref[:, planes - deepest :] * root_ref[planes - deepest :][None]


def second_filter_kernel(theirs, terms, rows, lanes, weight_ref, root_ref, own_ref, below_ref, above_ref,
                         out_ref, *rest):
    ext_ref = rest[-1]
    halves = out_ref.shape[1]
    load_extended(own_ref, below_ref, above_ref, root_ref, ext_ref, 0, rows)
    vec = lax.axis_index("vec")
    start = (1 - vec if theirs else vec) * halves

    def plane(i, _):
        def put(row, total):
            out_ref[:, i, pl.ds(row, 8)] = total

        filter_plane(ext_ref, weight_ref, root_ref, own_ref, 0, start + i, terms, rows, lanes, put)
        return 0

    lax.fori_loop(0, halves, plane, 0, unroll=4)


def gram_kernel(early, own_x_ref, other_x_ref, *refs):
    if early:
        ys, (out_ref, late_ref, acc_ref) = refs[:2], refs[2:]
        for place, ref in enumerate(ys):
            late_ref[pl.ds(place * chunk, chunk)] = ref[...]
    else:
        ys, (before_ref, out_ref, acc_ref) = refs[:4], refs[4:]
    cols = own_x_ref.shape[0]
    tiles = own_x_ref.shape[1] // 2
    group = chunk
    vec = lax.axis_index("vec")
    acc_ref[...] = jnp.zeros_like(acc_ref)

    def load(kind, number, t):
        if kind == "x":
            ref = own_x_ref if number < 2 else other_x_ref
            return [ref[(number % 2) * group + k, vec * tiles + t] for k in range(group)]
        return [ys[number][k, t] for k in range(group)]

    def block_of_pairs(slot, left_kind, left, right_kind, right):
        same = left == right
        pairs = [(i, j) for i in range(group) for j in range(group) if not (same and j < i)]

        def step(t, accs):
            a = load(left_kind, left, t)
            b = a if same and left_kind == right_kind else load(right_kind, right, t)
            return tuple(acc + a[i] * b[j] for (i, j), acc in zip(pairs, accs))

        zero = tuple(jnp.zeros((8, 128), f32) for _ in pairs)
        accs = lax.fori_loop(0, tiles, step, zero, unroll=4)
        for (i, j), acc in zip(pairs, accs):
            row = jnp.sum(acc, axis=0, keepdims=True)
            gi = lax.rem(left * group + i + cols * vec, 2 * cols)
            gj = lax.rem(right * group + j + cols * vec, 2 * cols)
            acc_ref[slot, pl.ds(gi * 16 + gj, 1), :] = row
            acc_ref[slot, pl.ds(gj * 16 + gi, 1), :] = row

    for left in range(4):
        for right in range(left, 4):
            if early:
                block_of_pairs(0, "x", left, "x", right)
            if (right < 2) == early:
                block_of_pairs(2, "y", left, "y", right)
                if left // 2 == right // 2:
                    block_of_pairs(1, "y", left, "x", right)
            if left // 2 != right // 2:
                if early:

                    @pl.when(vec == 0)
                    def _(left=left, right=right):
                        block_of_pairs(1, "y", left, "x", right)

                else:

                    @pl.when(vec == 1)
                    def _(left=left, right=right):
                        block_of_pairs(1, "y", right, "x", left)

    lane = lax.broadcasted_iota(jnp.int32, (256, 128), 1)
    inner = lax.rem(lax.broadcasted_iota(jnp.int32, (256, 128), 0), 16)
    total = jnp.zeros((16, 128), f32) if early else before_ref[...]
    for slot in range(0 if early else 1, 3):
        sums = jnp.sum(acc_ref[slot], axis=1, keepdims=True)
        placed = jnp.where(lane == inner + 16 * slot, sums, 0.0)
        total = total + jnp.sum(placed.reshape(16, 16, 128), axis=1)
    out_ref[...] = total


def eliminate(square):
    n = square.shape[0]
    row = lax.broadcasted_iota(jnp.int32, (n, n), 0)
    col = lax.broadcasted_iota(jnp.int32, (n, n), 1)
    work = square
    inverse = jnp.where(row == col, 1.0, 0.0).astype(f32)
    columns = jnp.zeros((n, n), f32)
    pivots = jnp.zeros((n, n), f32)
    across = jnp.zeros((n, n), f32)
    for j in range(n):
        column = jnp.broadcast_to(work[:, j : j + 1], (n, n))
        pivot = jnp.broadcast_to(column[j : j + 1, :], (n, n))
        factor = jnp.where(row > j, column, 0.0) / pivot
        columns = jnp.where((col == j) & (row >= j), column, columns)
        pivots = jnp.where(row == j, pivot, pivots)
        across = jnp.where(col == j, pivot, across)
        inverse = inverse - factor * jnp.broadcast_to(inverse[j : j + 1, :], (n, n))
        work = work - factor * jnp.broadcast_to(work[j : j + 1, :], (n, n))
    return columns * inverse_root(across), inverse * inverse_root(pivots)


def times(a, b):
    return jnp.dot(a, b, precision=highest, preferred_element_type=f32)


def times_t(a, b):
    return lax.dot_general(a, b, (((1,), (1,)), ((), ())), precision=highest, preferred_element_type=f32)


def algebra_kernel(scale, gram_ref, alpha_ref, beta_ref, table_ref):
    size = gram_ref.shape[0]
    _, inverse = eliminate(gram_ref[:, :size])
    half_way = times(inverse, gram_ref[...])
    both = jnp.concatenate([half_way[:, size : 2 * size], half_way[:, 2 * size : 3 * size]], axis=0)
    both = times_t(both, inverse)
    coeffs, image = both[:size], both[size:]
    factor, second = eliminate(image - times_t(coeffs, coeffs))
    alpha_ref[...] = coeffs
    beta_ref[...] = factor
    both = times(jnp.concatenate([times(second, coeffs), second], axis=0), inverse)
    of_start, of_image = -scale * both[:size], scale * both[size:]
    first = lax.axis_index("vec") == 0
    for place, mix in ((0, of_start), (16, of_image)):
        mine = jnp.where(first, mix[:8], mix[8:])
        table_ref[:, place : place + 8] = jnp.where(first, mine[:, :8], mine[:, 8:])
        table_ref[:, place + 8 : place + 16] = jnp.where(first, mine[:, 8:], mine[:, :8])


def combine_kernel(mine, table_ref, own_x_ref, other_x_ref, *refs):
    fields = [own_x_ref, other_x_ref]
    for ref in refs:
        if sum(field.shape[0] for field in fields) < table_ref.shape[1]:
            fields.append(ref)
    out_ref, block_ref, sem = refs[-3:]
    sources = [(ref, k) for ref in fields for k in range(ref.shape[0])]
    cols, tiles = block_ref.shape[:2]
    group = 8
    vec = lax.axis_index("vec")
    base = (vec if mine else 1 - vec) * tiles

    def copy(g):
        place = pl.multiple_of(g * group, group)
        return pltpu.make_async_copy(
            block_ref.at[:, pl.ds(place, group)], out_ref.at[:, pl.ds(base + place, group)], sem.at[g]
        )

    def step(g, _):
        first = pl.multiple_of(g * group, group)
        for i in range(cols):
            acc = None
            for j, (ref, k) in enumerate(sources):
                at = base + first if j < 2 * cols else first
                term = table_ref[i, j] * ref[k, pl.ds(at, group)]
                acc = term if acc is None else acc + term
            block_ref[i, pl.ds(first, group)] = acc
        copy(g).start()
        return 0

    lax.fori_loop(0, tiles // group, step, 0)
    for g in range(tiles // group):
        copy(g).wait()


def brick_of(zl, x, y, c):
    return ((zl * 4 + x) * 4 + y) * 2 + c


def places():
    for zl in range(2):
        for x in range(4):
            for y in range(4):
                for c in range(2):
                    yield brick_of(zl, x, y, c), zl, x, y, c


def crowded(zl, x, y):
    return (zl, x, y) in ((0, 0, 0), (1, 3, 3))


def swap_tables(half):
    direct, first, second = [], [], []
    detour = {0: ((1, 0), (3, 0)), 1: ((0, 1), (0, 3))}
    for brick, zl, x, y, c in places():
        for vec in range(2):
            here, there = brick * 2 + vec, brick * 2 + 1 - vec
            if not crowded(zl, x, y):
                direct.append((here, there))
                continue
            dx, dy = detour[c][half]
            relay = brick_of(zl, (x + dx) % 4, (y + dy) % 4, c) * 2 + 1 - vec
            first.append((here, relay))
            second.append((relay, there))
    return direct, first, second


def sum_everywhere(value):
    def moved(place, dim, by):
        _, zl, x, y, c = place
        if dim == "x":
            x = (x + by) % 4
        elif dim == "y":
            y = (y + by) % 4
        else:
            c = c ^ by
        return brick_of(zl, x, y, c)

    def permute(v, dim, by):
        return lax.ppermute(v, "brick", [(place[0], moved(place, dim, by)) for place in places()])

    value = value + permute(value, "core", 1)
    pairs = {}
    for by in (1, 2, 3):
        table = []
        for brick, zl, x, y, c in places():
            for vec in range(2):
                z = (2 * vec + zl + by) % 4
                table.append((brick * 2 + vec, brick_of(z % 2, x, y, c) * 2 + z // 2))
        pairs[by] = table
    near = [lax.ppermute(value, ("brick", "vec"), pairs[by]) for by in (1, 2, 3)]
    value = (value + near[0]) + (near[1] + near[2])
    for dim in ("y", "x"):
        near = [permute(value, dim, by) for by in (1, 2, 3)]
        value = (value + near[0]) + (near[1] + near[2])
    return value


def steps_of(levels, start_block):
    own_cols, planes, rows, lanes = start_block.shape
    bricks = lax.axis_size("brick")
    voxel_total = bricks * planes * rows * lanes
    halves = planes // 2
    upward = [(i, i + 1) for i in range(bricks - 1)]
    downward = [(i + 1, i) for i in range(bricks - 1)]
    swap = [(0, 1), (1, 0)]

    def up(value):
        return lax.ppermute(value, "brick", upward)

    def down(value):
        return lax.ppermute(value, "brick", downward)

    tail = pl.pallas_call(
        tail_kernel,
        out_shape=jax.ShapeDtypeStruct((sum(offsets_cube), rows, lanes), f32),
        in_specs=[HBM],
        out_specs=VMEM,
        scratch_shapes=[
            pltpu.VMEM((sum(offsets_cube), rows, lanes), jnp.int32),
            pltpu.SemaphoreType.DMA((len(offsets_cube),)),
        ],
        compiler_params=params(60),
        name="tail",
    )(levels)
    halo = up(tail)
    x_own = start_block.astype(f32)
    both = ("brick", "vec")
    x_relayed = []
    for half in range(2):
        direct, first_pairs, second_pairs = swap_tables(half)
        part = x_own[half * chunk : (half + 1) * chunk]
        part = lax.ppermute(part, both, first_pairs)
        x_relayed.append(lax.ppermute(part, both, second_pairs))
    x_other = lax.ppermute(x_own, both, direct)
    x_other = x_other + jnp.concatenate(x_relayed, axis=0)

    numbers = range(own_cols // chunk)
    edge = jax.ShapeDtypeStruct((chunk, deepest, rows, lanes), f32)
    root, *edges = pl.pallas_call(
        degree_kernel,
        out_shape=[jax.ShapeDtypeStruct((planes, rows, lanes), f32)] + [edge] * (2 * len(numbers)),
        in_specs=[VMEM] * 3,
        out_specs=[VMEM] * (1 + 2 * len(numbers)),
        compiler_params=params(4),
        name="degree",
    )(levels, halo, x_own)
    x_above, x_below = [], []
    for number in numbers:
        x_above.append(down(edges[2 * number]))
        x_below.append(up(edges[2 * number + 1]))

    terms = terms_of(rows, lanes)
    slots = len(terms)
    weights = pl.pallas_call(
        weights_kernel,
        out_shape=jax.ShapeDtypeStruct((slots, planes, rows, lanes), f32),
        in_specs=[VMEM] * 2,
        out_specs=VMEM,
        compiler_params=params(4),
        name="weights",
    )(levels, halo)
    ext = pltpu.VMEM((chunk, (planes + 2 * deepest) * rows, lanes), f32)

    def flat(value):
        return value.reshape(value.shape[0], -1, lanes)

    keep = jax.ShapeDtypeStruct(weights.shape, f32)

    def first_filter(number, weights):
        field = jax.ShapeDtypeStruct((chunk, planes, rows, lanes), f32)
        return pl.pallas_call(
            functools.partial(first_filter_kernel, number * chunk, terms, rows, lanes),
            out_shape=[field, edge, edge, keep],
            in_specs=[VMEM] * 5,
            out_specs=[VMEM] * 4,
            scratch_shapes=[ext],
            input_output_aliases={0: 3},
            compiler_params=params(8),
        )(weights, root, x_own, flat(x_below[number]), flat(x_above[number]))

    def second_filter(theirs, number, weights):
        return pl.pallas_call(
            functools.partial(second_filter_kernel, theirs, terms, rows, lanes),
            out_shape=[jax.ShapeDtypeStruct((chunk, halves, rows, lanes), f32), keep],
            in_specs=[VMEM] * 5,
            out_specs=[VMEM] * 2,
            scratch_shapes=[ext],
            input_output_aliases={0: 1},
            compiler_params=params(8),
        )(weights, root, fields[number], flat(belows[number]), flat(aboves[number]))

    fields, belows, aboves = [], [], []
    for number in numbers:
        field, low, high, weights = first_filter(number, weights)
        fields.append(field)
        aboves.append(down(low))
        belows.append(up(high))
    y_theirs, y_mine, y_other_mine = [], [], []
    for number in numbers:
        theirs, weights = second_filter(True, number, weights)
        y_theirs.append(theirs)
        y_other_mine.append(lax.ppermute(theirs, "vec", swap))
    for number in numbers:
        mine, weights = second_filter(False, number, weights)
        y_mine.append(mine)

    def tiled(value):
        return value.reshape(value.shape[0], -1, 8, lanes) if value.shape[2] != 8 else value

    def gram_call(early, *operands):
        out = jax.ShapeDtypeStruct((2 * own_cols, 128), f32)
        late = jax.ShapeDtypeStruct((own_cols, halves * rows // 8, 8, lanes), f32)
        return pl.pallas_call(
            functools.partial(gram_kernel, early),
            out_shape=(out, late) if early else out,
            in_specs=[VMEM] * len(operands),
            out_specs=(VMEM, VMEM) if early else VMEM,
            scratch_shapes=[pltpu.VMEM((3, 256, 128), f32)],
            compiler_params=params(4),
            name="gram_early" if early else "gram_late",
        )(*operands)

    mine_tiled = [tiled(value) for value in (x_own, x_other, *y_mine)]
    partial_gram, outgoing = gram_call(True, *mine_tiled)
    late = lax.ppermute(outgoing, "vec", [(0, 1)])
    gram = gram_call(False, *mine_tiled, *map(tiled, y_other_mine), partial_gram)
    gram = sum_everywhere(gram)

    small = jax.ShapeDtypeStruct((16, 16), f32)
    alpha, beta, table = pl.pallas_call(
        functools.partial(algebra_kernel, math.sqrt(voxel_total)),
        out_shape=[small, small, jax.ShapeDtypeStruct((own_cols, 4 * own_cols), f32)],
        in_specs=[VMEM],
        out_specs=[VMEM] * 3,
        compiler_params=params(4),
        name="algebra",
    )(gram)

    def combine(mine, *fields, before=None):
        half_tiles = halves * rows // 8
        extra = [] if before is None else [before]
        return pl.pallas_call(
            functools.partial(combine_kernel, mine),
            in_specs=[SMEM] + [VMEM] * len(fields) + [HBM] * len(extra),
            out_specs=HBM,
            out_shape=jax.ShapeDtypeStruct((own_cols, 2 * half_tiles, 8, lanes), f32),
            scratch_shapes=[
                pltpu.VMEM((own_cols, half_tiles, 8, lanes), f32),
                pltpu.SemaphoreType.DMA((half_tiles // 8,)),
            ],
            input_output_aliases={1 + len(fields): 0} if extra else {},
            compiler_params=params(4),
            name="combine_mine" if mine else "combine_theirs",
        )(table, *map(tiled, fields), *extra)

    basis = combine(True, x_own, x_other, *y_mine, *y_other_mine)
    basis = combine(False, x_own, x_other, *y_theirs, late, before=basis)
    return alpha[None], beta[None], basis.reshape(start_block.shape)


def solution(mesh):
    return jax.shard_map(
        steps_of,
        mesh=mesh,
        in_specs=(P(None, "brick", None, None), P("vec", "brick", None, None)),
        out_specs=(P(), P(), P("vec", "brick", None, None)),
        check_vma=False,
    )
```

```python
import functools
import math

import jax
import jax.numpy as jnp
from jax import lax
from jax.experimental import pallas as pl
from jax.experimental.pallas import tpu as pltpu
from jax.sharding import PartitionSpec as P


offsets_cube = (1, 3, 9, 27)
deepest = 27
highest = lax.Precision.HIGHEST
chunk = 4
f32 = jnp.float32


ANY = pl.BlockSpec(memory_space=pl.ANY)
SMEM = pl.BlockSpec(memory_space=pltpu.SMEM)
VMEM = pl.BlockSpec(memory_space=pltpu.VMEM)
HBM = pl.BlockSpec(memory_space=pltpu.HBM)


def params(mib):
    return pltpu.CompilerParams(vmem_limit_bytes=mib << 20)


def shift_rows(value, by):
    length = value.shape[-2]
    if abs(by) >= length:
        return jnp.zeros_like(value)
    rolled = pltpu.roll(value, (-by) % length, value.ndim - 2)
    row = lax.broadcasted_iota(jnp.int32, value.shape, value.ndim - 2) + by
    return jnp.where((row >= 0) & (row < length), rolled, 0.0)


def shift_lanes(value, by):
    length = value.shape[-1]
    if abs(by) >= length:
        return jnp.zeros_like(value)
    rolled = pltpu.roll(value, (-by) % length, value.ndim - 1)
    lane = lax.broadcasted_iota(jnp.int32, value.shape, value.ndim - 1) + by
    return jnp.where((lane >= 0) & (lane < length), rolled, 0.0)


def inverse_root(value):
    guess = lax.rsqrt(value)
    return guess * (1.5 - 0.5 * value * guess * guess)


def to_weight(level):
    return (level.astype(f32) + 0.5) / 256.0


def halo_start(position):
    return sum(offsets_cube[:position])


def tail_kernel(levels_ref, out_ref, raw_ref, sem):
    planes = levels_ref.shape[1]
    copies = []
    for position, offset in enumerate(offsets_cube):
        place = pl.ds(halo_start(position), offset)
        copies.append(
            pltpu.make_async_copy(
                levels_ref.at[position, pl.ds(planes - offset, offset)], raw_ref.at[place], sem.at[position]
            )
        )
    for copy in copies:
        copy.start()
    for copy in copies:
        copy.wait()
    out_ref[...] = to_weight(raw_ref[...])


def degree_kernel(levels_ref, halo_ref, start_ref, root_ref, *edge_refs):
    planes = levels_ref.shape[1]
    inside_above = (lax.axis_index("brick") < lax.axis_size("brick") - 1).astype(f32)

    def plane(x, _):
        total = jnp.ones(levels_ref.shape[2:], f32)
        for position, offset in enumerate(offsets_cube):
            weight = to_weight(levels_ref[position, x])
            total = total + jnp.where(x + offset < planes, 1.0, inside_above) * weight
            own = to_weight(levels_ref[position, jnp.maximum(x - offset, 0)])
            base = halo_start(position)
            far = halo_ref[base + jnp.minimum(x, offset - 1)]
            total = total + jnp.where(x >= offset, own, far)
            for axis, shift in ((1, shift_rows), (2, shift_lanes)):
                weight = to_weight(levels_ref[4 * axis + position, x])
                ones = shift(jnp.ones_like(weight), offset)
                total = total + ones * weight + shift(weight, -offset)
        root_ref[x] = inverse_root(total)
        return 0

    lax.fori_loop(0, planes, plane, 0, unroll=4)
    for number in range(len(edge_refs) // 2):
        low_ref, high_ref = edge_refs[2 * number : 2 * number + 2]

        def edge(x, _, number=number, low_ref=low_ref, high_ref=high_ref):
            for ref, far in ((low_ref, x), (high_ref, x + planes - deepest)):
                ref[:, x] = start_ref[pl.ds(number * chunk, chunk), far] * root_ref[far][None]
            return 0

        lax.fori_loop(0, deepest, edge, 0, unroll=3)


def weights_kernel(levels_ref, halo_ref, out_ref):
    planes = levels_ref.shape[1]

    def plane(x, _):
        slot = 0
        for position, offset in enumerate(offsets_cube):
            out_ref[slot, x] = to_weight(levels_ref[position, x])
            own = to_weight(levels_ref[position, jnp.maximum(x - offset, 0)])
            far = halo_ref[halo_start(position) + jnp.minimum(x, offset - 1)]
            out_ref[slot + 1, x] = jnp.where(x >= offset, own, far)
            slot += 2
        for axis, shift in ((1, shift_rows), (2, shift_lanes)):
            for position, offset in enumerate(offsets_cube):
                if offset >= levels_ref.shape[axis + 1]:
                    continue
                weight = to_weight(levels_ref[4 * axis + position, x])
                forward = weight * shift(jnp.ones_like(weight), offset)
                out_ref[slot, x] = forward
                out_ref[slot + 1, x] = shift(forward, -offset)
                slot += 2
        return 0

    lax.fori_loop(0, planes, plane, 0, unroll=4)


def terms_of(rows, lanes):
    found = [("x", o * s) for o in offsets_cube for s in (1, -1)]
    found += [("y", o * s) for o in offsets_cube if o < rows for s in (1, -1)]
    found += [("z", o * s) for o in offsets_cube if o < lanes for s in (1, -1)]
    return found


def filter_plane(ext_ref, weight_ref, root_ref, own_ref, first, x, terms, rows, lanes, put):
    for row in range(0, rows, 8):
        base = pl.multiple_of((x + deepest) * rows + row, 8)
        here = ext_ref[:, pl.ds(base, 8), :]
        total = None
        for slot, (kind, by) in enumerate(terms):
            weight = weight_ref[slot, x, pl.ds(row, 8)]
            if kind == "x":
                moved = ext_ref[:, pl.ds(base + by * rows, 8), :]
            elif kind == "y":
                moved = ext_ref[:, pl.ds(base + by, 8), :]
            else:
                moved = pltpu.roll(here, (-by) % lanes, 2)
            term = weight[None] * moved
            total = term if total is None else total + term
        own = own_ref[pl.ds(first, ext_ref.shape[0]), x, pl.ds(row, 8)]
        put(row, 0.5 * (own + root_ref[x, pl.ds(row, 8)][None] * total))


def load_extended(own_ref, below_ref, above_ref, root_ref, ext_ref, first, rows):
    count = ext_ref.shape[0]
    planes = root_ref.shape[0]
    edge = deepest * rows
    ext_ref[:, pl.ds(0, edge)] = below_ref[...]
    ext_ref[:, pl.ds(edge + planes * rows, edge)] = above_ref[...]

    def plane(x, _):
        place = pl.ds(pl.multiple_of(edge + x * rows, rows), rows)
        ext_ref[:, place] = own_ref[pl.ds(first, count), x] * root_ref[x][None]
        return 0

    lax.fori_loop(0, planes, plane, 0, unroll=4)


def first_filter_kernel(first, terms, rows, lanes, weight_ref, root_ref, own_ref, below_ref, above_ref,
                        out_ref, low_ref, high_ref, *rest):
    ext_ref = rest[-1]
    planes = weight_ref.shape[1]
    load_extended(own_ref, below_ref, above_ref, root_ref, ext_ref, first, rows)

    def plane(x, _):
        def put(row, total):
            out_ref[:, x, pl.ds(row, 8)] = total

        filter_plane(ext_ref, weight_ref, root_ref, own_ref, first, x, terms, rows, lanes, put)
        return 0

    lax.fori_loop(0, planes, plane, 0, unroll=4)
    low_ref[...] = out_ref[:, :deepest] * root_ref[:deepest][None]
    high_ref[...] = out_ref[:, planes - deepest :] * root_ref[planes - deepest :][None]


def second_filter_kernel(theirs, terms, rows, lanes, weight_ref, root_ref, own_ref, below_ref, above_ref,
                         out_ref, *rest):
    ext_ref = rest[-1]
    halves = out_ref.shape[1]
    load_extended(own_ref, below_ref, above_ref, root_ref, ext_ref, 0, rows)
    vec = lax.axis_index("vec")
    start = (1 - vec if theirs else vec) * halves

    def plane(i, _):
        def put(row, total):
            out_ref[:, i, pl.ds(row, 8)] = total

        filter_plane(ext_ref, weight_ref, root_ref, own_ref, 0, start + i, terms, rows, lanes, put)
        return 0

    lax.fori_loop(0, halves, plane, 0, unroll=4)


def gram_kernel(early, own_x_ref, other_x_ref, *refs):
    if early:
        ys, (out_ref, late_ref, acc_ref) = refs[:2], refs[2:]
        for place, ref in enumerate(ys):
            late_ref[pl.ds(place * chunk, chunk)] = ref[...]
    else:
        ys, (before_ref, out_ref, acc_ref) = refs[:4], refs[4:]
    cols = own_x_ref.shape[0]
    tiles = own_x_ref.shape[1] // 2
    group = chunk
    vec = lax.axis_index("vec")
    acc_ref[...] = jnp.zeros_like(acc_ref)

    def load(kind, number, t):
        if kind == "x":
            ref = own_x_ref if number < 2 else other_x_ref
            return [ref[(number % 2) * group + k, vec * tiles + t] for k in range(group)]
        return [ys[number][k, t] for k in range(group)]

    def block_of_pairs(slot, left_kind, left, right_kind, right):
        same = left == right
        pairs = [(i, j) for i in range(group) for j in range(group) if not (same and j < i)]

        def step(t, accs):
            a = load(left_kind, left, t)
            b = a if same and left_kind == right_kind else load(right_kind, right, t)
            return tuple(acc + a[i] * b[j] for (i, j), acc in zip(pairs, accs))

        zero = tuple(jnp.zeros((8, 128), f32) for _ in pairs)
        accs = lax.fori_loop(0, tiles, step, zero, unroll=4)
        for (i, j), acc in zip(pairs, accs):
            row = jnp.sum(acc, axis=0, keepdims=True)
            gi = lax.rem(left * group + i + cols * vec, 2 * cols)
            gj = lax.rem(right * group + j + cols * vec, 2 * cols)
            acc_ref[slot, pl.ds(gi * 16 + gj, 1), :] = row
            acc_ref[slot, pl.ds(gj * 16 + gi, 1), :] = row

    for left in range(4):
        for right in range(left, 4):
            if early:
                block_of_pairs(0, "x", left, "x", right)
            if (right < 2) == early:
                block_of_pairs(2, "y", left, "y", right)
                if left // 2 == right // 2:
                    block_of_pairs(1, "y", left, "x", right)
            if left // 2 != right // 2:
                if early:

                    @pl.when(vec == 0)
                    def _(left=left, right=right):
                        block_of_pairs(1, "y", left, "x", right)

                else:

                    @pl.when(vec == 1)
                    def _(left=left, right=right):
                        block_of_pairs(1, "y", right, "x", left)

    lane = lax.broadcasted_iota(jnp.int32, (256, 128), 1)
    inner = lax.rem(lax.broadcasted_iota(jnp.int32, (256, 128), 0), 16)
    total = jnp.zeros((16, 128), f32) if early else before_ref[...]
    for slot in range(0 if early else 1, 3):
        sums = jnp.sum(acc_ref[slot], axis=1, keepdims=True)
        placed = jnp.where(lane == inner + 16 * slot, sums, 0.0)
        total = total + jnp.sum(placed.reshape(16, 16, 128), axis=1)
    out_ref[...] = total


def eliminate(square):
    n = square.shape[0]
    row = lax.broadcasted_iota(jnp.int32, (n, n), 0)
    col = lax.broadcasted_iota(jnp.int32, (n, n), 1)
    work = square
    inverse = jnp.where(row == col, 1.0, 0.0).astype(f32)
    columns = jnp.zeros((n, n), f32)
    pivots = jnp.zeros((n, n), f32)
    across = jnp.zeros((n, n), f32)
    for j in range(n):
        column = jnp.broadcast_to(work[:, j : j + 1], (n, n))
        pivot = jnp.broadcast_to(column[j : j + 1, :], (n, n))
        factor = jnp.where(row > j, column, 0.0) / pivot
        columns = jnp.where((col == j) & (row >= j), column, columns)
        pivots = jnp.where(row == j, pivot, pivots)
        across = jnp.where(col == j, pivot, across)
        inverse = inverse - factor * jnp.broadcast_to(inverse[j : j + 1, :], (n, n))
        work = work - factor * jnp.broadcast_to(work[j : j + 1, :], (n, n))
    return columns * inverse_root(across), inverse * inverse_root(pivots)


def times(a, b):
    return jnp.dot(a, b, precision=highest, preferred_element_type=f32)


def times_t(a, b):
    return lax.dot_general(a, b, (((1,), (1,)), ((), ())), precision=highest, preferred_element_type=f32)


def algebra_kernel(scale, gram_ref, alpha_ref, beta_ref, table_ref):
    size = gram_ref.shape[0]
    _, inverse = eliminate(gram_ref[:, :size])
    half_way = times(inverse, gram_ref[...])
    both = jnp.concatenate([half_way[:, size : 2 * size], half_way[:, 2 * size : 3 * size]], axis=0)
    both = times_t(both, inverse)
    coeffs, image = both[:size], both[size:]
    factor, second = eliminate(image - times_t(coeffs, coeffs))
    alpha_ref[...] = coeffs
    beta_ref[...] = factor
    both = times(jnp.concatenate([times(second, coeffs), second], axis=0), inverse)
    of_start, of_image = -scale * both[:size], scale * both[size:]
    first = lax.axis_index("vec") == 0
    for place, mix in ((0, of_start), (16, of_image)):
        mine = jnp.where(first, mix[:8], mix[8:])
        for part, half in enumerate((jnp.where(first, mine[:, :8], mine[:, 8:]), jnp.where(first, mine[:, 8:], mine[:, :8]))):
            for j in range(8):
                table_ref[place + 8 * part + j] = jnp.broadcast_to(half[:, j : j + 1], table_ref.shape[1:])


def combine_kernel(mine, table_ref, own_x_ref, other_x_ref, *refs):
    fields = [own_x_ref, other_x_ref]
    for ref in refs:
        if sum(field.shape[0] for field in fields) < table_ref.shape[0]:
            fields.append(ref)
    out_ref, block_ref, sem = refs[-3:]
    sources = [(ref, k) for ref in fields for k in range(ref.shape[0])]
    cols, tiles = block_ref.shape[:2]
    group = 8
    vec = lax.axis_index("vec")
    base = (vec if mine else 1 - vec) * tiles

    def copy(g):
        place = pl.multiple_of(g * group, group)
        return pltpu.make_async_copy(
            block_ref.at[:, pl.ds(place, group)], out_ref.at[:, pl.ds(base + place, group)], sem.at[g]
        )

    def step(g, _):
        first = pl.multiple_of(g * group, group)
        for i in range(cols):
            acc = None
            for j, (ref, k) in enumerate(sources):
                at = base + first if j < 2 * cols else first
                factor = jnp.broadcast_to(table_ref[j, pl.ds(i, 1)], table_ref.shape[1:])
                term = factor[None] * ref[k, pl.ds(at, group)]
                acc = term if acc is None else acc + term
            block_ref[i, pl.ds(first, group)] = acc
        copy(g).start()
        return 0

    lax.fori_loop(0, tiles // group, step, 0)
    for g in range(tiles // group):
        copy(g).wait()


def brick_of(zl, x, y, c):
    return ((zl * 4 + x) * 4 + y) * 2 + c


def places():
    for zl in range(2):
        for x in range(4):
            for y in range(4):
                for c in range(2):
                    yield brick_of(zl, x, y, c), zl, x, y, c


def crowded(zl, x, y):
    return (zl, x, y) in ((0, 0, 0), (1, 3, 3))


def swap_tables(half):
    direct, first, second = [], [], []
    detour = {0: ((1, 0), (3, 0)), 1: ((0, 1), (0, 3))}
    for brick, zl, x, y, c in places():
        for vec in range(2):
            here, there = brick * 2 + vec, brick * 2 + 1 - vec
            if not crowded(zl, x, y):
                direct.append((here, there))
                continue
            dx, dy = detour[c][half]
            relay = brick_of(zl, (x + dx) % 4, (y + dy) % 4, c) * 2 + 1 - vec
            first.append((here, relay))
            second.append((relay, there))
    return direct, first, second


def sum_everywhere(value):
    def moved(place, dim, by):
        _, zl, x, y, c = place
        if dim == "x":
            x = (x + by) % 4
        elif dim == "y":
            y = (y + by) % 4
        else:
            c = c ^ by
        return brick_of(zl, x, y, c)

    def permute(v, dim, by):
        return lax.ppermute(v, "brick", [(place[0], moved(place, dim, by)) for place in places()])

    value = value + permute(value, "core", 1)
    pairs = {}
    for by in (1, 2, 3):
        table = []
        for brick, zl, x, y, c in places():
            for vec in range(2):
                z = (2 * vec + zl + by) % 4
                table.append((brick * 2 + vec, brick_of(z % 2, x, y, c) * 2 + z // 2))
        pairs[by] = table
    near = [lax.ppermute(value, ("brick", "vec"), pairs[by]) for by in (1, 2, 3)]
    value = (value + near[0]) + (near[1] + near[2])
    for dim in ("y", "x"):
        near = [permute(value, dim, by) for by in (1, 2, 3)]
        value = (value + near[0]) + (near[1] + near[2])
    return value


def steps_of(levels, start_block):
    own_cols, planes, rows, lanes = start_block.shape
    bricks = lax.axis_size("brick")
    voxel_total = bricks * planes * rows * lanes
    halves = planes // 2
    upward = [(i, i + 1) for i in range(bricks - 1)]
    downward = [(i + 1, i) for i in range(bricks - 1)]
    swap = [(0, 1), (1, 0)]

    def up(value):
        return lax.ppermute(value, "brick", upward)

    def down(value):
        return lax.ppermute(value, "brick", downward)

    tail = pl.pallas_call(
        tail_kernel,
        out_shape=jax.ShapeDtypeStruct((sum(offsets_cube), rows, lanes), f32),
        in_specs=[HBM],
        out_specs=VMEM,
        scratch_shapes=[
            pltpu.VMEM((sum(offsets_cube), rows, lanes), jnp.int32),
            pltpu.SemaphoreType.DMA((len(offsets_cube),)),
        ],
        compiler_params=params(60),
        name="tail",
    )(levels)
    halo = up(tail)
    x_own = start_block.astype(f32)
    both = ("brick", "vec")
    x_relayed = []
    for half in range(2):
        direct, first_pairs, second_pairs = swap_tables(half)
        part = x_own[half * chunk : (half + 1) * chunk]
        part = lax.ppermute(part, both, first_pairs)
        x_relayed.append(lax.ppermute(part, both, second_pairs))
    x_other = lax.ppermute(x_own, both, direct)
    x_other = x_other + jnp.concatenate(x_relayed, axis=0)

    numbers = range(own_cols // chunk)
    edge = jax.ShapeDtypeStruct((chunk, deepest, rows, lanes), f32)
    root, *edges = pl.pallas_call(
        degree_kernel,
        out_shape=[jax.ShapeDtypeStruct((planes, rows, lanes), f32)] + [edge] * (2 * len(numbers)),
        in_specs=[VMEM] * 3,
        out_specs=[VMEM] * (1 + 2 * len(numbers)),
        compiler_params=params(4),
        name="degree",
    )(levels, halo, x_own)
    x_above, x_below = [], []
    for number in numbers:
        x_above.append(down(edges[2 * number]))
        x_below.append(up(edges[2 * number + 1]))

    terms = terms_of(rows, lanes)
    slots = len(terms)
    weights = pl.pallas_call(
        weights_kernel,
        out_shape=jax.ShapeDtypeStruct((slots, planes, rows, lanes), f32),
        in_specs=[VMEM] * 2,
        out_specs=VMEM,
        compiler_params=params(4),
        name="weights",
    )(levels, halo)
    ext = pltpu.VMEM((chunk, (planes + 2 * deepest) * rows, lanes), f32)

    def flat(value):
        return value.reshape(value.shape[0], -1, lanes)

    keep = jax.ShapeDtypeStruct(weights.shape, f32)

    def first_filter(number, weights):
        field = jax.ShapeDtypeStruct((chunk, planes, rows, lanes), f32)
        return pl.pallas_call(
            functools.partial(first_filter_kernel, number * chunk, terms, rows, lanes),
            out_shape=[field, edge, edge, keep],
            in_specs=[VMEM] * 5,
            out_specs=[VMEM] * 4,
            scratch_shapes=[ext],
            input_output_aliases={0: 3},
            compiler_params=params(8),
        )(weights, root, x_own, flat(x_below[number]), flat(x_above[number]))

    def second_filter(theirs, number, weights):
        return pl.pallas_call(
            functools.partial(second_filter_kernel, theirs, terms, rows, lanes),
            out_shape=[jax.ShapeDtypeStruct((chunk, halves, rows, lanes), f32), keep],
            in_specs=[VMEM] * 5,
            out_specs=[VMEM] * 2,
            scratch_shapes=[ext],
            input_output_aliases={0: 1},
            compiler_params=params(8),
        )(weights, root, fields[number], flat(belows[number]), flat(aboves[number]))

    fields, belows, aboves = [], [], []
    for number in numbers:
        field, low, high, weights = first_filter(number, weights)
        fields.append(field)
        aboves.append(down(low))
        belows.append(up(high))
    y_theirs, y_mine, y_other_mine = [], [], []
    for number in numbers:
        theirs, weights = second_filter(True, number, weights)
        y_theirs.append(theirs)
        y_other_mine.append(lax.ppermute(theirs, "vec", swap))
    for number in numbers:
        mine, weights = second_filter(False, number, weights)
        y_mine.append(mine)

    def tiled(value):
        return value.reshape(value.shape[0], -1, 8, lanes) if value.shape[2] != 8 else value

    def gram_call(early, *operands):
        out = jax.ShapeDtypeStruct((2 * own_cols, 128), f32)
        late = jax.ShapeDtypeStruct((own_cols, halves * rows // 8, 8, lanes), f32)
        return pl.pallas_call(
            functools.partial(gram_kernel, early),
            out_shape=(out, late) if early else out,
            in_specs=[VMEM] * len(operands),
            out_specs=(VMEM, VMEM) if early else VMEM,
            scratch_shapes=[pltpu.VMEM((3, 256, 128), f32)],
            compiler_params=params(4),
            name="gram_early" if early else "gram_late",
        )(*operands)

    mine_tiled = [tiled(value) for value in (x_own, x_other, *y_mine)]
    partial_gram, outgoing = gram_call(True, *mine_tiled)
    late = lax.ppermute(outgoing, "vec", [(0, 1)])
    gram = gram_call(False, *mine_tiled, *map(tiled, y_other_mine), partial_gram)
    gram = sum_everywhere(gram)

    small = jax.ShapeDtypeStruct((16, 16), f32)
    alpha, beta, table = pl.pallas_call(
        functools.partial(algebra_kernel, math.sqrt(voxel_total)),
        out_shape=[small, small, jax.ShapeDtypeStruct((4 * own_cols, own_cols, lanes), f32)],
        in_specs=[VMEM],
        out_specs=[VMEM] * 3,
        compiler_params=params(4),
        name="algebra",
    )(gram)

    def combine(mine, *fields, before=None):
        half_tiles = halves * rows // 8
        extra = [] if before is None else [before]
        return pl.pallas_call(
            functools.partial(combine_kernel, mine),
            in_specs=[VMEM] * (1 + len(fields)) + [HBM] * len(extra),
            out_specs=HBM,
            out_shape=jax.ShapeDtypeStruct((own_cols, 2 * half_tiles, 8, lanes), f32),
            scratch_shapes=[
                pltpu.VMEM((own_cols, half_tiles, 8, lanes), f32),
                pltpu.SemaphoreType.DMA((half_tiles // 8,)),
            ],
            input_output_aliases={1 + len(fields): 0} if extra else {},
            compiler_params=params(4),
            name="combine_mine" if mine else "combine_theirs",
        )(table, *map(tiled, fields), *extra)

    basis = combine(True, x_own, x_other, *y_mine, *y_other_mine)
    basis = combine(False, x_own, x_other, *y_theirs, late, before=basis)
    return alpha[None], beta[None], basis.reshape(start_block.shape)


def solution(mesh):
    return jax.shard_map(
        steps_of,
        mesh=mesh,
        in_specs=(P(None, "brick", None, None), P("vec", "brick", None, None)),
        out_specs=(P(), P(), P("vec", "brick", None, None)),
        check_vma=False,
    )
```

```python
import functools
import math

import jax
import jax.numpy as jnp
from jax import lax
from jax.experimental import pallas as pl
from jax.experimental.pallas import tpu as pltpu
from jax.sharding import PartitionSpec as P


offsets_cube = (1, 3, 9, 27)
deepest = 27
highest = lax.Precision.HIGHEST
chunk = 4
f32 = jnp.float32


ANY = pl.BlockSpec(memory_space=pl.ANY)
SMEM = pl.BlockSpec(memory_space=pltpu.SMEM)
VMEM = pl.BlockSpec(memory_space=pltpu.VMEM)
HBM = pl.BlockSpec(memory_space=pltpu.HBM)


def params(mib):
    return pltpu.CompilerParams(vmem_limit_bytes=mib << 20)


def shift_rows(value, by):
    length = value.shape[-2]
    if abs(by) >= length:
        return jnp.zeros_like(value)
    rolled = pltpu.roll(value, (-by) % length, value.ndim - 2)
    row = lax.broadcasted_iota(jnp.int32, value.shape, value.ndim - 2) + by
    return jnp.where((row >= 0) & (row < length), rolled, 0.0)


def shift_lanes(value, by):
    length = value.shape[-1]
    if abs(by) >= length:
        return jnp.zeros_like(value)
    rolled = pltpu.roll(value, (-by) % length, value.ndim - 1)
    lane = lax.broadcasted_iota(jnp.int32, value.shape, value.ndim - 1) + by
    return jnp.where((lane >= 0) & (lane < length), rolled, 0.0)


def inverse_root(value):
    guess = lax.rsqrt(value)
    return guess * (1.5 - 0.5 * value * guess * guess)


def to_weight(level):
    return (level.astype(f32) + 0.5) / 256.0


def halo_start(position):
    return sum(offsets_cube[:position])


def tail_kernel(levels_ref, out_ref, raw_ref, sem):
    planes = levels_ref.shape[1]
    copies = []
    for position, offset in enumerate(offsets_cube):
        place = pl.ds(halo_start(position), offset)
        copies.append(
            pltpu.make_async_copy(
                levels_ref.at[position, pl.ds(planes - offset, offset)], raw_ref.at[place], sem.at[position]
            )
        )
    for copy in copies:
        copy.start()
    for copy in copies:
        copy.wait()
    out_ref[...] = to_weight(raw_ref[...])


def degree_kernel(levels_ref, halo_ref, start_ref, root_ref, *edge_refs):
    planes = levels_ref.shape[1]
    inside_above = (lax.axis_index("brick") < lax.axis_size("brick") - 1).astype(f32)

    def plane(x, _):
        total = jnp.ones(levels_ref.shape[2:], f32)
        for position, offset in enumerate(offsets_cube):
            weight = to_weight(levels_ref[position, x])
            total = total + jnp.where(x + offset < planes, 1.0, inside_above) * weight
            own = to_weight(levels_ref[position, jnp.maximum(x - offset, 0)])
            base = halo_start(position)
            far = halo_ref[base + jnp.minimum(x, offset - 1)]
            total = total + jnp.where(x >= offset, own, far)
            for axis, shift in ((1, shift_rows), (2, shift_lanes)):
                weight = to_weight(levels_ref[4 * axis + position, x])
                ones = shift(jnp.ones_like(weight), offset)
                total = total + ones * weight + shift(weight, -offset)
        root_ref[x] = inverse_root(total)
        return 0

    lax.fori_loop(0, planes, plane, 0, unroll=4)
    for number in range(len(edge_refs) // 2):
        low_ref, high_ref = edge_refs[2 * number : 2 * number + 2]

        def edge(x, _, number=number, low_ref=low_ref, high_ref=high_ref):
            for ref, far in ((low_ref, x), (high_ref, x + planes - deepest)):
                ref[:, x] = start_ref[pl.ds(number * chunk, chunk), far] * root_ref[far][None]
            return 0

        lax.fori_loop(0, deepest, edge, 0, unroll=3)


def weights_kernel(levels_ref, halo_ref, out_ref):
    planes = levels_ref.shape[1]

    def plane(x, _):
        slot = 0
        for position, offset in enumerate(offsets_cube):
            out_ref[slot, x] = to_weight(levels_ref[position, x])
            own = to_weight(levels_ref[position, jnp.maximum(x - offset, 0)])
            far = halo_ref[halo_start(position) + jnp.minimum(x, offset - 1)]
            out_ref[slot + 1, x] = jnp.where(x >= offset, own, far)
            slot += 2
        for axis, shift in ((1, shift_rows), (2, shift_lanes)):
            for position, offset in enumerate(offsets_cube):
                if offset >= levels_ref.shape[axis + 1]:
                    continue
                weight = to_weight(levels_ref[4 * axis + position, x])
                forward = weight * shift(jnp.ones_like(weight), offset)
                out_ref[slot, x] = forward
                out_ref[slot + 1, x] = shift(forward, -offset)
                slot += 2
        return 0

    lax.fori_loop(0, planes, plane, 0, unroll=4)


def terms_of(rows, lanes):
    found = [("x", o * s) for o in offsets_cube for s in (1, -1)]
    found += [("y", o * s) for o in offsets_cube if o < rows for s in (1, -1)]
    found += [("z", o * s) for o in offsets_cube if o < lanes for s in (1, -1)]
    return found


def filter_plane(ext_ref, weight_ref, root_ref, own_ref, first, x, terms, rows, lanes, put):
    for row in range(0, rows, 8):
        base = pl.multiple_of((x + deepest) * rows + row, 8)
        here = ext_ref[:, pl.ds(base, 8), :]
        total = None
        for slot, (kind, by) in enumerate(terms):
            weight = weight_ref[slot, x, pl.ds(row, 8)]
            if kind == "x":
                moved = ext_ref[:, pl.ds(base + by * rows, 8), :]
            elif kind == "y":
                moved = ext_ref[:, pl.ds(base + by, 8), :]
            else:
                moved = pltpu.roll(here, (-by) % lanes, 2)
            term = weight[None] * moved
            total = term if total is None else total + term
        own = own_ref[pl.ds(first, ext_ref.shape[0]), x, pl.ds(row, 8)]
        put(row, 0.5 * (own + root_ref[x, pl.ds(row, 8)][None] * total))


def load_extended(own_ref, below_ref, above_ref, root_ref, ext_ref, first, rows):
    count = ext_ref.shape[0]
    planes = root_ref.shape[0]
    edge = deepest * rows
    ext_ref[:, pl.ds(0, edge)] = below_ref[...]
    ext_ref[:, pl.ds(edge + planes * rows, edge)] = above_ref[...]

    def plane(x, _):
        place = pl.ds(pl.multiple_of(edge + x * rows, rows), rows)
        ext_ref[:, place] = own_ref[pl.ds(first, count), x] * root_ref[x][None]
        return 0

    lax.fori_loop(0, planes, plane, 0, unroll=4)


def first_filter_kernel(first, terms, rows, lanes, weight_ref, root_ref, own_ref, below_ref, above_ref,
                        out_ref, low_ref, high_ref, *rest):
    ext_ref = rest[-1]
    planes = weight_ref.shape[1]
    load_extended(own_ref, below_ref, above_ref, root_ref, ext_ref, first, rows)

    def plane(x, _):
        def put(row, total):
            out_ref[:, x, pl.ds(row, 8)] = total

        filter_plane(ext_ref, weight_ref, root_ref, own_ref, first, x, terms, rows, lanes, put)
        return 0

    lax.fori_loop(0, planes, plane, 0, unroll=4)
    low_ref[...] = out_ref[:, :deepest] * root_ref[:deepest][None]
    high_ref[...] = out_ref[:, planes - deepest :] * root_ref[planes - deepest :][None]


def second_filter_kernel(theirs, terms, rows, lanes, weight_ref, root_ref, own_ref, below_ref, above_ref,
                         out_ref, *rest):
    ext_ref = rest[-1]
    halves = out_ref.shape[1]
    load_extended(own_ref, below_ref, above_ref, root_ref, ext_ref, 0, rows)
    vec = lax.axis_index("vec")
    start = (1 - vec if theirs else vec) * halves

    def plane(i, _):
        def put(row, total):
            out_ref[:, i, pl.ds(row, 8)] = total

        filter_plane(ext_ref, weight_ref, root_ref, own_ref, 0, start + i, terms, rows, lanes, put)
        return 0

    lax.fori_loop(0, halves, plane, 0, unroll=4)


def gram_kernel(early, own_x_ref, other_x_ref, *refs):
    if early:
        ys, (out_ref, late_ref, acc_ref) = refs[:2], refs[2:]
        for place, ref in enumerate(ys):
            late_ref[pl.ds(place * chunk, chunk)] = ref[...]
    else:
        ys, (before_ref, out_ref, acc_ref) = refs[:4], refs[4:]
    cols = own_x_ref.shape[0]
    tiles = own_x_ref.shape[1] // 2
    group = chunk
    vec = lax.axis_index("vec")
    acc_ref[...] = jnp.zeros_like(acc_ref)

    def load(kind, number, t):
        if kind == "x":
            ref = own_x_ref if number < 2 else other_x_ref
            return [ref[(number % 2) * group + k, vec * tiles + t] for k in range(group)]
        return [ys[number][k, t] for k in range(group)]

    def block_of_pairs(slot, left_kind, left, right_kind, right):
        same = left == right
        pairs = [(i, j) for i in range(group) for j in range(group) if not (same and j < i)]

        def step(t, accs):
            a = load(left_kind, left, t)
            b = a if same and left_kind == right_kind else load(right_kind, right, t)
            return tuple(acc + a[i] * b[j] for (i, j), acc in zip(pairs, accs))

        zero = tuple(jnp.zeros((8, 128), f32) for _ in pairs)
        accs = lax.fori_loop(0, tiles, step, zero, unroll=4)
        for (i, j), acc in zip(pairs, accs):
            row = jnp.sum(acc, axis=0, keepdims=True)
            gi = lax.rem(left * group + i + cols * vec, 2 * cols)
            gj = lax.rem(right * group + j + cols * vec, 2 * cols)
            acc_ref[slot, pl.ds(gi * 16 + gj, 1), :] = row
            acc_ref[slot, pl.ds(gj * 16 + gi, 1), :] = row

    for left in range(4):
        for right in range(left, 4):
            if early:
                block_of_pairs(0, "x", left, "x", right)
            if (right < 2) == early:
                if left // 2 == right // 2:
                    block_of_pairs(1, "y", left, "x", right)
            if left // 2 != right // 2:
                if early:

                    @pl.when(vec == 0)
                    def _(left=left, right=right):
                        block_of_pairs(1, "y", left, "x", right)

                else:

                    @pl.when(vec == 1)
                    def _(left=left, right=right):
                        block_of_pairs(1, "y", right, "x", left)

    lane = lax.broadcasted_iota(jnp.int32, (256, 128), 1)
    inner = lax.rem(lax.broadcasted_iota(jnp.int32, (256, 128), 0), 16)
    total = jnp.zeros((16, 128), f32) if early else before_ref[...]
    for slot in range(0 if early else 1, 2):
        sums = jnp.sum(acc_ref[slot], axis=1, keepdims=True)
        placed = jnp.where(lane == inner + 16 * slot, sums, 0.0)
        total = total + jnp.sum(placed.reshape(16, 16, 128), axis=1)
    out_ref[...] = total


def eliminate(square):
    n = square.shape[0]
    row = lax.broadcasted_iota(jnp.int32, (n, n), 0)
    col = lax.broadcasted_iota(jnp.int32, (n, n), 1)
    work = square
    inverse = jnp.where(row == col, 1.0, 0.0).astype(f32)
    columns = jnp.zeros((n, n), f32)
    pivots = jnp.zeros((n, n), f32)
    across = jnp.zeros((n, n), f32)
    for j in range(n):
        column = jnp.broadcast_to(work[:, j : j + 1], (n, n))
        pivot = jnp.broadcast_to(column[j : j + 1, :], (n, n))
        factor = jnp.where(row > j, column, 0.0) / pivot
        columns = jnp.where((col == j) & (row >= j), column, columns)
        pivots = jnp.where(row == j, pivot, pivots)
        across = jnp.where(col == j, pivot, across)
        inverse = inverse - factor * jnp.broadcast_to(inverse[j : j + 1, :], (n, n))
        work = work - factor * jnp.broadcast_to(work[j : j + 1, :], (n, n))
    return columns * inverse_root(across), inverse * inverse_root(pivots)


def times(a, b):
    return jnp.dot(a, b, precision=highest, preferred_element_type=f32)


def times_t(a, b):
    return lax.dot_general(a, b, (((1,), (1,)), ((), ())), precision=highest, preferred_element_type=f32)


def project_kernel(gram_ref, alpha_ref, inverse_ref, mix_ref, table_ref):
    size = gram_ref.shape[0]
    _, inverse = eliminate(gram_ref[:, :size])
    image = gram_ref[:, size : 2 * size]
    right = times_t(image, inverse)
    alpha_ref[...] = times(inverse, right)
    inverse_ref[...] = inverse
    mix = times(right, inverse)
    mix_ref[...] = mix
    first = lax.axis_index("vec") == 0
    rows = jnp.where(first, mix, jnp.concatenate([mix[8:], mix[:8]], axis=0))
    for j in range(size):
        column = jnp.where(first, rows[:, j : j + 1], rows[:, (j + 8) % size : (j + 8) % size + 1])
        table_ref[j] = jnp.broadcast_to(column, table_ref.shape[1:])


def residual_kernel(table_ref, own_x_ref, other_x_ref, *refs):
    ys, (out_ref, rest_ref, acc_ref) = refs[:4], refs[4:]
    cols = own_x_ref.shape[0]
    tiles = rest_ref.shape[1]
    group = 8
    vec = lax.axis_index("vec")
    xs = [(ref, k) for ref in (own_x_ref, other_x_ref) for k in range(cols)]

    def subtract(g, _):
        first = pl.multiple_of(g * group, group)
        for i in range(2 * cols):
            acc = ys[i // chunk][i % chunk, pl.ds(first, group)]
            for j, (ref, k) in enumerate(xs):
                factor = jnp.broadcast_to(table_ref[j, pl.ds(i, 1)], (8, 128))
                acc = acc - factor[None] * ref[k, pl.ds(vec * tiles + first, group)]
            rest_ref[i, pl.ds(first, group)] = acc
        return 0

    lax.fori_loop(0, tiles // group, subtract, 0)
    for left in range(0, 2 * cols, chunk):
        for right in range(left, 2 * cols, chunk):
            pairs = [(i, j) for i in range(left, left + chunk) for j in range(right, right + chunk) if i <= j]

            def step(t, accs, pairs=pairs, left=left, right=right):
                a = {i: rest_ref[i, t] for i in sorted({*range(left, left + chunk), *range(right, right + chunk)})}
                return tuple(acc + a[i] * a[j] for (i, j), acc in zip(pairs, accs))

            accs = lax.fori_loop(0, tiles, step, tuple(jnp.zeros((8, 128), f32) for _ in pairs), unroll=4)
            for (i, j), acc in zip(pairs, accs):
                row = jnp.sum(acc, axis=0, keepdims=True)
                gi = lax.rem(i + cols * vec, 2 * cols)
                gj = lax.rem(j + cols * vec, 2 * cols)
                acc_ref[pl.ds(gi * 16 + gj, 1), :] = row
                acc_ref[pl.ds(gj * 16 + gi, 1), :] = row
    lane = lax.broadcasted_iota(jnp.int32, (256, 128), 1)
    inner = lax.rem(lax.broadcasted_iota(jnp.int32, (256, 128), 0), 16)
    sums = jnp.sum(acc_ref[...], axis=1, keepdims=True)
    out_ref[...] = jnp.sum(jnp.where(lane == inner, sums, 0.0).reshape(16, 16, 128), axis=1)


def algebra_kernel(scale, gram_ref, inverse_ref, mix_ref, beta_ref, table_ref):
    inverse = inverse_ref[...]
    factor, second = eliminate(times_t(times(inverse, gram_ref[:, :16]), inverse))
    beta_ref[...] = factor
    of_image = scale * times(second, inverse)
    of_start = -times(of_image, mix_ref[...])
    first = lax.axis_index("vec") == 0
    for place, mix in ((0, of_start), (16, of_image)):
        mine = jnp.where(first, mix[:8], mix[8:])
        for part, half in enumerate((jnp.where(first, mine[:, :8], mine[:, 8:]), jnp.where(first, mine[:, 8:], mine[:, :8]))):
            for j in range(8):
                table_ref[place + 8 * part + j] = jnp.broadcast_to(half[:, j : j + 1], table_ref.shape[1:])


def combine_kernel(mine, table_ref, own_x_ref, other_x_ref, *refs):
    fields = [own_x_ref, other_x_ref]
    for ref in refs:
        if sum(field.shape[0] for field in fields) < table_ref.shape[0]:
            fields.append(ref)
    out_ref, block_ref, sem = refs[-3:]
    sources = [(ref, k) for ref in fields for k in range(ref.shape[0])]
    cols, tiles = block_ref.shape[:2]
    group = 8
    vec = lax.axis_index("vec")
    base = (vec if mine else 1 - vec) * tiles

    def copy(g):
        place = pl.multiple_of(g * group, group)
        return pltpu.make_async_copy(
            block_ref.at[:, pl.ds(place, group)], out_ref.at[:, pl.ds(base + place, group)], sem.at[g]
        )

    def step(g, _):
        first = pl.multiple_of(g * group, group)
        for i in range(cols):
            acc = None
            for j, (ref, k) in enumerate(sources):
                at = base + first if j < 2 * cols else first
                factor = jnp.broadcast_to(table_ref[j, pl.ds(i, 1)], table_ref.shape[1:])
                term = factor[None] * ref[k, pl.ds(at, group)]
                acc = term if acc is None else acc + term
            block_ref[i, pl.ds(first, group)] = acc
        copy(g).start()
        return 0

    lax.fori_loop(0, tiles // group, step, 0)
    for g in range(tiles // group):
        copy(g).wait()


def brick_of(zl, x, y, c):
    return ((zl * 4 + x) * 4 + y) * 2 + c


def places():
    for zl in range(2):
        for x in range(4):
            for y in range(4):
                for c in range(2):
                    yield brick_of(zl, x, y, c), zl, x, y, c


def crowded(zl, x, y):
    return (zl, x, y) in ((0, 0, 0), (1, 3, 3))


def swap_tables(half):
    direct, first, second = [], [], []
    detour = {0: ((1, 0), (3, 0)), 1: ((0, 1), (0, 3))}
    for brick, zl, x, y, c in places():
        for vec in range(2):
            here, there = brick * 2 + vec, brick * 2 + 1 - vec
            if not crowded(zl, x, y):
                direct.append((here, there))
                continue
            dx, dy = detour[c][half]
            relay = brick_of(zl, (x + dx) % 4, (y + dy) % 4, c) * 2 + 1 - vec
            first.append((here, relay))
            second.append((relay, there))
    return direct, first, second


def sum_everywhere(value):
    def moved(place, dim, by):
        _, zl, x, y, c = place
        if dim == "x":
            x = (x + by) % 4
        elif dim == "y":
            y = (y + by) % 4
        else:
            c = c ^ by
        return brick_of(zl, x, y, c)

    def permute(v, dim, by):
        return lax.ppermute(v, "brick", [(place[0], moved(place, dim, by)) for place in places()])

    value = value + permute(value, "core", 1)
    pairs = {}
    for by in (1, 2, 3):
        table = []
        for brick, zl, x, y, c in places():
            for vec in range(2):
                z = (2 * vec + zl + by) % 4
                table.append((brick * 2 + vec, brick_of(z % 2, x, y, c) * 2 + z // 2))
        pairs[by] = table
    near = [lax.ppermute(value, ("brick", "vec"), pairs[by]) for by in (1, 2, 3)]
    value = (value + near[0]) + (near[1] + near[2])
    for dim in ("y", "x"):
        near = [permute(value, dim, by) for by in (1, 2, 3)]
        value = (value + near[0]) + (near[1] + near[2])
    return value


def steps_of(levels, start_block):
    own_cols, planes, rows, lanes = start_block.shape
    bricks = lax.axis_size("brick")
    voxel_total = bricks * planes * rows * lanes
    halves = planes // 2
    upward = [(i, i + 1) for i in range(bricks - 1)]
    downward = [(i + 1, i) for i in range(bricks - 1)]
    swap = [(0, 1), (1, 0)]

    def up(value):
        return lax.ppermute(value, "brick", upward)

    def down(value):
        return lax.ppermute(value, "brick", downward)

    tail = pl.pallas_call(
        tail_kernel,
        out_shape=jax.ShapeDtypeStruct((sum(offsets_cube), rows, lanes), f32),
        in_specs=[HBM],
        out_specs=VMEM,
        scratch_shapes=[
            pltpu.VMEM((sum(offsets_cube), rows, lanes), jnp.int32),
            pltpu.SemaphoreType.DMA((len(offsets_cube),)),
        ],
        compiler_params=params(60),
        name="tail",
    )(levels)
    halo = up(tail)
    x_own = start_block.astype(f32)
    both = ("brick", "vec")
    x_relayed = []
    for half in range(2):
        direct, first_pairs, second_pairs = swap_tables(half)
        part = x_own[half * chunk : (half + 1) * chunk]
        part = lax.ppermute(part, both, first_pairs)
        x_relayed.append(lax.ppermute(part, both, second_pairs))
    x_other = lax.ppermute(x_own, both, direct)
    x_other = x_other + jnp.concatenate(x_relayed, axis=0)

    numbers = range(own_cols // chunk)
    edge = jax.ShapeDtypeStruct((chunk, deepest, rows, lanes), f32)
    root, *edges = pl.pallas_call(
        degree_kernel,
        out_shape=[jax.ShapeDtypeStruct((planes, rows, lanes), f32)] + [edge] * (2 * len(numbers)),
        in_specs=[VMEM] * 3,
        out_specs=[VMEM] * (1 + 2 * len(numbers)),
        compiler_params=params(4),
        name="degree",
    )(levels, halo, x_own)
    x_above, x_below = [], []
    for number in numbers:
        x_above.append(down(edges[2 * number]))
        x_below.append(up(edges[2 * number + 1]))

    terms = terms_of(rows, lanes)
    slots = len(terms)
    weights = pl.pallas_call(
        weights_kernel,
        out_shape=jax.ShapeDtypeStruct((slots, planes, rows, lanes), f32),
        in_specs=[VMEM] * 2,
        out_specs=VMEM,
        compiler_params=params(4),
        name="weights",
    )(levels, halo)
    ext = pltpu.VMEM((chunk, (planes + 2 * deepest) * rows, lanes), f32)

    def flat(value):
        return value.reshape(value.shape[0], -1, lanes)

    keep = jax.ShapeDtypeStruct(weights.shape, f32)

    def first_filter(number, weights):
        field = jax.ShapeDtypeStruct((chunk, planes, rows, lanes), f32)
        return pl.pallas_call(
            functools.partial(first_filter_kernel, number * chunk, terms, rows, lanes),
            out_shape=[field, edge, edge, keep],
            in_specs=[VMEM] * 5,
            out_specs=[VMEM] * 4,
            scratch_shapes=[ext],
            input_output_aliases={0: 3},
            compiler_params=params(8),
        )(weights, root, x_own, flat(x_below[number]), flat(x_above[number]))

    def second_filter(theirs, number, weights):
        return pl.pallas_call(
            functools.partial(second_filter_kernel, theirs, terms, rows, lanes),
            out_shape=[jax.ShapeDtypeStruct((chunk, halves, rows, lanes), f32), keep],
            in_specs=[VMEM] * 5,
            out_specs=[VMEM] * 2,
            scratch_shapes=[ext],
            input_output_aliases={0: 1},
            compiler_params=params(8),
        )(weights, root, fields[number], flat(belows[number]), flat(aboves[number]))

    fields, belows, aboves = [], [], []
    for number in numbers:
        field, low, high, weights = first_filter(number, weights)
        fields.append(field)
        aboves.append(down(low))
        belows.append(up(high))
    y_theirs, y_mine, y_other_mine = [], [], []
    for number in numbers:
        theirs, weights = second_filter(True, number, weights)
        y_theirs.append(theirs)
        y_other_mine.append(lax.ppermute(theirs, "vec", swap))
    for number in numbers:
        mine, weights = second_filter(False, number, weights)
        y_mine.append(mine)

    def tiled(value):
        return value.reshape(value.shape[0], -1, 8, lanes) if value.shape[2] != 8 else value

    def gram_call(early, *operands):
        out = jax.ShapeDtypeStruct((2 * own_cols, 128), f32)
        late = jax.ShapeDtypeStruct((own_cols, halves * rows // 8, 8, lanes), f32)
        return pl.pallas_call(
            functools.partial(gram_kernel, early),
            out_shape=(out, late) if early else out,
            in_specs=[VMEM] * len(operands),
            out_specs=(VMEM, VMEM) if early else VMEM,
            scratch_shapes=[pltpu.VMEM((2, 256, 128), f32)],
            compiler_params=params(4),
            name="gram_early" if early else "gram_late",
        )(*operands)

    mine_tiled = [tiled(value) for value in (x_own, x_other, *y_mine)]
    partial_gram, outgoing = gram_call(True, *mine_tiled)
    late = lax.ppermute(outgoing, "vec", [(0, 1)])
    gram = gram_call(False, *mine_tiled, *map(tiled, y_other_mine), partial_gram)
    gram = sum_everywhere(gram)

    small = jax.ShapeDtypeStruct((16, 16), f32)
    alpha, inverse, mix, project = pl.pallas_call(
        project_kernel,
        out_shape=[small, small, small, jax.ShapeDtypeStruct((2 * own_cols, 2 * own_cols, lanes), f32)],
        in_specs=[VMEM],
        out_specs=[VMEM] * 4,
        compiler_params=params(4),
        name="project",
    )(gram)
    rest_gram = pl.pallas_call(
        residual_kernel,
        out_shape=jax.ShapeDtypeStruct((2 * own_cols, 128), f32),
        in_specs=[VMEM] * 7,
        out_specs=VMEM,
        scratch_shapes=[
            pltpu.VMEM((2 * own_cols, halves * rows // 8, 8, lanes), f32),
            pltpu.VMEM((256, 128), f32),
        ],
        compiler_params=params(6),
        name="residual",
    )(project, *mine_tiled, *map(tiled, y_other_mine))
    rest_gram = sum_everywhere(rest_gram)
    beta, table = pl.pallas_call(
        functools.partial(algebra_kernel, math.sqrt(voxel_total)),
        out_shape=[small, jax.ShapeDtypeStruct((4 * own_cols, own_cols, lanes), f32)],
        in_specs=[VMEM] * 3,
        out_specs=[VMEM] * 2,
        compiler_params=params(4),
        name="algebra",
    )(rest_gram, inverse, mix)

    def combine(mine, *fields, before=None):
        half_tiles = halves * rows // 8
        extra = [] if before is None else [before]
        return pl.pallas_call(
            functools.partial(combine_kernel, mine),
            in_specs=[VMEM] * (1 + len(fields)) + [HBM] * len(extra),
            out_specs=HBM,
            out_shape=jax.ShapeDtypeStruct((own_cols, 2 * half_tiles, 8, lanes), f32),
            scratch_shapes=[
                pltpu.VMEM((own_cols, half_tiles, 8, lanes), f32),
                pltpu.SemaphoreType.DMA((half_tiles // 8,)),
            ],
            input_output_aliases={1 + len(fields): 0} if extra else {},
            compiler_params=params(4),
            name="combine_mine" if mine else "combine_theirs",
        )(table, *map(tiled, fields), *extra)

    basis = combine(True, x_own, x_other, *y_mine, *y_other_mine)
    basis = combine(False, x_own, x_other, *y_theirs, late, before=basis)
    return alpha[None], beta[None], basis.reshape(start_block.shape)


def solution(mesh):
    return jax.shard_map(
        steps_of,
        mesh=mesh,
        in_specs=(P(None, "brick", None, None), P("vec", "brick", None, None)),
        out_specs=(P(), P(), P("vec", "brick", None, None)),
        check_vma=False,
    )
```

```python
import functools
import math

import jax
import jax.numpy as jnp
from jax import lax
from jax.experimental import pallas as pl
from jax.experimental.pallas import tpu as pltpu
from jax.sharding import PartitionSpec as P


offsets_cube = (1, 3, 9, 27)
deepest = 27
highest = lax.Precision.HIGHEST
chunk = 4
f32 = jnp.float32


ANY = pl.BlockSpec(memory_space=pl.ANY)
SMEM = pl.BlockSpec(memory_space=pltpu.SMEM)
VMEM = pl.BlockSpec(memory_space=pltpu.VMEM)
HBM = pl.BlockSpec(memory_space=pltpu.HBM)


def params(mib):
    return pltpu.CompilerParams(vmem_limit_bytes=mib << 20)


def shift_rows(value, by):
    length = value.shape[-2]
    if abs(by) >= length:
        return jnp.zeros_like(value)
    rolled = pltpu.roll(value, (-by) % length, value.ndim - 2)
    row = lax.broadcasted_iota(jnp.int32, value.shape, value.ndim - 2) + by
    return jnp.where((row >= 0) & (row < length), rolled, 0.0)


def shift_lanes(value, by):
    length = value.shape[-1]
    if abs(by) >= length:
        return jnp.zeros_like(value)
    rolled = pltpu.roll(value, (-by) % length, value.ndim - 1)
    lane = lax.broadcasted_iota(jnp.int32, value.shape, value.ndim - 1) + by
    return jnp.where((lane >= 0) & (lane < length), rolled, 0.0)


def inverse_root(value):
    guess = lax.rsqrt(value)
    return guess * (1.5 - 0.5 * value * guess * guess)


def to_weight(level):
    return (level.astype(f32) + 0.5) / 256.0


def halo_start(position):
    return sum(offsets_cube[:position])


def tail_kernel(levels_ref, out_ref, raw_ref, sem):
    planes = levels_ref.shape[1]
    copies = []
    for position, offset in enumerate(offsets_cube):
        place = pl.ds(halo_start(position), offset)
        copies.append(
            pltpu.make_async_copy(
                levels_ref.at[position, pl.ds(planes - offset, offset)], raw_ref.at[place], sem.at[position]
            )
        )
    for copy in copies:
        copy.start()
    for copy in copies:
        copy.wait()
    out_ref[...] = to_weight(raw_ref[...])


def degree_kernel(levels_ref, halo_ref, start_ref, root_ref, *edge_refs):
    planes = levels_ref.shape[1]
    inside_above = (lax.axis_index("brick") < lax.axis_size("brick") - 1).astype(f32)

    def plane(x, _):
        total = jnp.ones(levels_ref.shape[2:], f32)
        for position, offset in enumerate(offsets_cube):
            weight = to_weight(levels_ref[position, x])
            total = total + jnp.where(x + offset < planes, 1.0, inside_above) * weight
            own = to_weight(levels_ref[position, jnp.maximum(x - offset, 0)])
            base = halo_start(position)
            far = halo_ref[base + jnp.minimum(x, offset - 1)]
            total = total + jnp.where(x >= offset, own, far)
            for axis, shift in ((1, shift_rows), (2, shift_lanes)):
                weight = to_weight(levels_ref[4 * axis + position, x])
                ones = shift(jnp.ones_like(weight), offset)
                total = total + ones * weight + shift(weight, -offset)
        root_ref[x] = inverse_root(total)
        return 0

    lax.fori_loop(0, planes, plane, 0, unroll=4)
    for number in range(len(edge_refs) // 2):
        low_ref, high_ref = edge_refs[2 * number : 2 * number + 2]

        def edge(x, _, number=number, low_ref=low_ref, high_ref=high_ref):
            for ref, far in ((low_ref, x), (high_ref, x + planes - deepest)):
                ref[:, x] = start_ref[pl.ds(number * chunk, chunk), far] * root_ref[far][None]
            return 0

        lax.fori_loop(0, deepest, edge, 0, unroll=3)


def weights_kernel(levels_ref, halo_ref, out_ref):
    planes = levels_ref.shape[1]

    def plane(x, _):
        slot = 0
        for position, offset in enumerate(offsets_cube):
            out_ref[slot, x] = to_weight(levels_ref[position, x])
            own = to_weight(levels_ref[position, jnp.maximum(x - offset, 0)])
            far = halo_ref[halo_start(position) + jnp.minimum(x, offset - 1)]
            out_ref[slot + 1, x] = jnp.where(x >= offset, own, far)
            slot += 2
        for axis, shift in ((1, shift_rows), (2, shift_lanes)):
            for position, offset in enumerate(offsets_cube):
                if offset >= levels_ref.shape[axis + 1]:
                    continue
                weight = to_weight(levels_ref[4 * axis + position, x])
                forward = weight * shift(jnp.ones_like(weight), offset)
                out_ref[slot, x] = forward
                out_ref[slot + 1, x] = shift(forward, -offset)
                slot += 2
        return 0

    lax.fori_loop(0, planes, plane, 0, unroll=4)


def terms_of(rows, lanes):
    found = [("x", o * s) for o in offsets_cube for s in (1, -1)]
    found += [("y", o * s) for o in offsets_cube if o < rows for s in (1, -1)]
    found += [("z", o * s) for o in offsets_cube if o < lanes for s in (1, -1)]
    return found


def filter_plane(ext_ref, weight_ref, root_ref, own_ref, first, x, terms, rows, lanes, put):
    for row in range(0, rows, 8):
        base = pl.multiple_of((x + deepest) * rows + row, 8)
        here = ext_ref[:, pl.ds(base, 8), :]
        total = None
        for slot, (kind, by) in enumerate(terms):
            weight = weight_ref[slot, x, pl.ds(row, 8)]
            if kind == "x":
                moved = ext_ref[:, pl.ds(base + by * rows, 8), :]
            elif kind == "y":
                moved = ext_ref[:, pl.ds(base + by, 8), :]
            else:
                moved = pltpu.roll(here, (-by) % lanes, 2)
            term = weight[None] * moved
            total = term if total is None else total + term
        own = own_ref[pl.ds(first, ext_ref.shape[0]), x, pl.ds(row, 8)]
        put(row, 0.5 * (own + root_ref[x, pl.ds(row, 8)][None] * total))


def load_extended(own_ref, below_ref, above_ref, root_ref, ext_ref, first, rows):
    count = ext_ref.shape[0]
    planes = root_ref.shape[0]
    edge = deepest * rows
    ext_ref[:, pl.ds(0, edge)] = below_ref[...]
    ext_ref[:, pl.ds(edge + planes * rows, edge)] = above_ref[...]

    def plane(x, _):
        place = pl.ds(pl.multiple_of(edge + x * rows, rows), rows)
        ext_ref[:, place] = own_ref[pl.ds(first, count), x] * root_ref[x][None]
        return 0

    lax.fori_loop(0, planes, plane, 0, unroll=4)


def first_filter_kernel(first, terms, rows, lanes, weight_ref, root_ref, own_ref, below_ref, above_ref,
                        out_ref, low_ref, high_ref, *rest):
    ext_ref = rest[-1]
    planes = weight_ref.shape[1]
    load_extended(own_ref, below_ref, above_ref, root_ref, ext_ref, first, rows)

    def plane(x, _):
        def put(row, total):
            out_ref[:, x, pl.ds(row, 8)] = total

        filter_plane(ext_ref, weight_ref, root_ref, own_ref, first, x, terms, rows, lanes, put)
        return 0

    lax.fori_loop(0, planes, plane, 0, unroll=4)
    low_ref[...] = out_ref[:, :deepest] * root_ref[:deepest][None]
    high_ref[...] = out_ref[:, planes - deepest :] * root_ref[planes - deepest :][None]


def second_filter_kernel(theirs, terms, rows, lanes, weight_ref, root_ref, own_ref, below_ref, above_ref,
                         out_ref, *rest):
    ext_ref = rest[-1]
    halves = out_ref.shape[1]
    load_extended(own_ref, below_ref, above_ref, root_ref, ext_ref, 0, rows)
    vec = lax.axis_index("vec")
    start = (1 - vec if theirs else vec) * halves

    def plane(i, _):
        def put(row, total):
            out_ref[:, i, pl.ds(row, 8)] = total

        filter_plane(ext_ref, weight_ref, root_ref, own_ref, 0, start + i, terms, rows, lanes, put)
        return 0

    lax.fori_loop(0, halves, plane, 0, unroll=4)


def gram_kernel(own_x_ref, other_x_ref, *refs):
    ys, (out_ref, late_ref, acc_ref) = refs[:4], refs[4:]
    for place, ref in enumerate(ys[2:]):
        late_ref[pl.ds(place * chunk, chunk)] = ref[...]
    cols = own_x_ref.shape[0]
    tiles = own_x_ref.shape[1] // 2
    vec = lax.axis_index("vec")
    acc_ref[...] = jnp.zeros_like(acc_ref)

    def xs(number, tile):
        ref = own_x_ref if number < 2 else other_x_ref
        return [ref[(number % 2) * chunk + k, tile] for k in range(chunk)]

    def place_of(number, k):
        return lax.rem(number * chunk + k + cols * vec, 2 * cols)

    for left in range(4):
        for right in range(4):
            pairs = [(i, j) for i in range(chunk) for j in range(chunk)]
            zero = tuple(jnp.zeros((8, 128), f32) for _ in pairs)
            if right >= left:

                def step(t, accs):
                    a, b = xs(left, vec * tiles + t), xs(right, vec * tiles + t)
                    return tuple(acc + a[i] * b[j] for (i, j), acc in zip(pairs, accs))

                for (i, j), acc in zip(pairs, lax.fori_loop(0, tiles, step, zero, unroll=4)):
                    row = jnp.sum(acc, axis=0, keepdims=True)
                    gi, gj = place_of(left, i), place_of(right, j)
                    acc_ref[0, pl.ds(gi * 16 + gj, 1), :] = row
                    acc_ref[0, pl.ds(gj * 16 + gi, 1), :] = row
            if left < 2:
                accs = zero
                for first, y_ref in (((1 - vec) * tiles, ys[left]), (vec * tiles, ys[2 + left])):

                    def step_y(t, accs, first=first, y_ref=y_ref):
                        b = xs(right, first + t)
                        return tuple(acc + y_ref[i, t] * b[j] for (i, j), acc in zip(pairs, accs))

                    accs = lax.fori_loop(0, tiles, step_y, accs, unroll=4)
                for (i, j), acc in zip(pairs, accs):
                    at = place_of(left, i) * 16 + place_of(right, j)
                    acc_ref[1, pl.ds(at, 1), :] = jnp.sum(acc, axis=0, keepdims=True)

    lane = lax.broadcasted_iota(jnp.int32, (256, 128), 1)
    inner = lax.rem(lax.broadcasted_iota(jnp.int32, (256, 128), 0), 16)
    total = jnp.zeros((16, 128), f32)
    for slot in range(2):
        sums = jnp.sum(acc_ref[slot], axis=1, keepdims=True)
        placed = jnp.where(lane == inner + 16 * slot, sums, 0.0)
        total = total + jnp.sum(placed.reshape(16, 16, 128), axis=1)
    out_ref[...] = total


def eliminate(square):
    n = square.shape[0]
    row = lax.broadcasted_iota(jnp.int32, (n, n), 0)
    col = lax.broadcasted_iota(jnp.int32, (n, n), 1)
    work = square
    inverse = jnp.where(row == col, 1.0, 0.0).astype(f32)
    columns = jnp.zeros((n, n), f32)
    pivots = jnp.zeros((n, n), f32)
    across = jnp.zeros((n, n), f32)
    for j in range(n):
        column = jnp.broadcast_to(work[:, j : j + 1], (n, n))
        pivot = jnp.broadcast_to(column[j : j + 1, :], (n, n))
        factor = jnp.where(row > j, column, 0.0) / pivot
        columns = jnp.where((col == j) & (row >= j), column, columns)
        pivots = jnp.where(row == j, pivot, pivots)
        across = jnp.where(col == j, pivot, across)
        inverse = inverse - factor * jnp.broadcast_to(inverse[j : j + 1, :], (n, n))
        work = work - factor * jnp.broadcast_to(work[j : j + 1, :], (n, n))
    return columns * inverse_root(across), inverse * inverse_root(pivots)


def times(a, b):
    return jnp.dot(a, b, precision=highest, preferred_element_type=f32)


def times_t(a, b):
    return lax.dot_general(a, b, (((1,), (1,)), ((), ())), precision=highest, preferred_element_type=f32)


def project_kernel(gram_ref, alpha_ref, inverse_ref, mix_ref, table_ref):
    size = gram_ref.shape[0]
    _, inverse = eliminate(gram_ref[:, :size])
    image = gram_ref[:, size : 2 * size]
    right = times_t(image, inverse)
    alpha_ref[...] = times(inverse, right)
    inverse_ref[...] = inverse
    mix = times(right, inverse)
    mix_ref[...] = mix
    first = lax.axis_index("vec") == 0
    rows = jnp.where(first, mix, jnp.concatenate([mix[8:], mix[:8]], axis=0))
    for j in range(size):
        column = jnp.where(first, rows[:, j : j + 1], rows[:, (j + 8) % size : (j + 8) % size + 1])
        table_ref[j] = jnp.broadcast_to(column, table_ref.shape[1:])


def residual_kernel(table_ref, own_x_ref, other_x_ref, *refs):
    ys, (out_ref, rest_ref, acc_ref) = refs[:4], refs[4:]
    cols = own_x_ref.shape[0]
    tiles = rest_ref.shape[1]
    group = 8
    vec = lax.axis_index("vec")
    xs = [(ref, k) for ref in (own_x_ref, other_x_ref) for k in range(cols)]

    def subtract(g, _):
        first = pl.multiple_of(g * group, group)
        for i in range(2 * cols):
            acc = ys[i // chunk][i % chunk, pl.ds(first, group)]
            for j, (ref, k) in enumerate(xs):
                factor = jnp.broadcast_to(table_ref[j, pl.ds(i, 1)], (8, 128))
                acc = acc - factor[None] * ref[k, pl.ds(vec * tiles + first, group)]
            rest_ref[i, pl.ds(first, group)] = acc
        return 0

    lax.fori_loop(0, tiles // group, subtract, 0)
    for left in range(0, 2 * cols, chunk):
        for right in range(left, 2 * cols, chunk):
            pairs = [(i, j) for i in range(left, left + chunk) for j in range(right, right + chunk) if i <= j]

            def step(t, accs, pairs=pairs, left=left, right=right):
                a = {i: rest_ref[i, t] for i in sorted({*range(left, left + chunk), *range(right, right + chunk)})}
                return tuple(acc + a[i] * a[j] for (i, j), acc in zip(pairs, accs))

            accs = lax.fori_loop(0, tiles, step, tuple(jnp.zeros((8, 128), f32) for _ in pairs), unroll=4)
            for (i, j), acc in zip(pairs, accs):
                row = jnp.sum(acc, axis=0, keepdims=True)
                gi = lax.rem(i + cols * vec, 2 * cols)
                gj = lax.rem(j + cols * vec, 2 * cols)
                acc_ref[pl.ds(gi * 16 + gj, 1), :] = row
                acc_ref[pl.ds(gj * 16 + gi, 1), :] = row
    lane = lax.broadcasted_iota(jnp.int32, (256, 128), 1)
    inner = lax.rem(lax.broadcasted_iota(jnp.int32, (256, 128), 0), 16)
    sums = jnp.sum(acc_ref[...], axis=1, keepdims=True)
    out_ref[...] = jnp.sum(jnp.where(lane == inner, sums, 0.0).reshape(16, 16, 128), axis=1)


def algebra_kernel(scale, gram_ref, inverse_ref, mix_ref, beta_ref, table_ref):
    inverse = inverse_ref[...]
    factor, second = eliminate(times_t(times(inverse, gram_ref[:, :16]), inverse))
    beta_ref[...] = factor
    of_image = scale * times(second, inverse)
    of_start = -times(of_image, mix_ref[...])
    first = lax.axis_index("vec") == 0
    for place, mix in ((0, of_start), (16, of_image)):
        mine = jnp.where(first, mix[:8], mix[8:])
        for part, half in enumerate((jnp.where(first, mine[:, :8], mine[:, 8:]), jnp.where(first, mine[:, 8:], mine[:, :8]))):
            for j in range(8):
                table_ref[place + 8 * part + j] = jnp.broadcast_to(half[:, j : j + 1], table_ref.shape[1:])


def combine_kernel(mine, table_ref, own_x_ref, other_x_ref, *refs):
    fields = [own_x_ref, other_x_ref]
    for ref in refs:
        if sum(field.shape[0] for field in fields) < table_ref.shape[0]:
            fields.append(ref)
    out_ref, block_ref, sem = refs[-3:]
    sources = [(ref, k) for ref in fields for k in range(ref.shape[0])]
    cols, tiles = block_ref.shape[:2]
    group = 8
    vec = lax.axis_index("vec")
    base = (vec if mine else 1 - vec) * tiles

    def copy(g):
        place = pl.multiple_of(g * group, group)
        return pltpu.make_async_copy(
            block_ref.at[:, pl.ds(place, group)], out_ref.at[:, pl.ds(base + place, group)], sem.at[g]
        )

    def step(g, _):
        first = pl.multiple_of(g * group, group)
        for i in range(cols):
            acc = None
            for j, (ref, k) in enumerate(sources):
                at = base + first if j < 2 * cols else first
                factor = jnp.broadcast_to(table_ref[j, pl.ds(i, 1)], table_ref.shape[1:])
                term = factor[None] * ref[k, pl.ds(at, group)]
                acc = term if acc is None else acc + term
            block_ref[i, pl.ds(first, group)] = acc
        copy(g).start()
        return 0

    lax.fori_loop(0, tiles // group, step, 0)
    for g in range(tiles // group):
        copy(g).wait()


def brick_of(zl, x, y, c):
    return ((zl * 4 + x) * 4 + y) * 2 + c


def places():
    for zl in range(2):
        for x in range(4):
            for y in range(4):
                for c in range(2):
                    yield brick_of(zl, x, y, c), zl, x, y, c


def crowded(zl, x, y):
    return (zl, x, y) in ((0, 0, 0), (1, 3, 3))


def swap_tables(half):
    direct, first, second = [], [], []
    detour = {0: ((1, 0), (3, 0)), 1: ((0, 1), (0, 3))}
    for brick, zl, x, y, c in places():
        for vec in range(2):
            here, there = brick * 2 + vec, brick * 2 + 1 - vec
            if not crowded(zl, x, y):
                direct.append((here, there))
                continue
            dx, dy = detour[c][half]
            relay = brick_of(zl, (x + dx) % 4, (y + dy) % 4, c) * 2 + 1 - vec
            first.append((here, relay))
            second.append((relay, there))
    return direct, first, second


def sum_everywhere(value):
    def moved(place, dim, by):
        _, zl, x, y, c = place
        if dim == "x":
            x = (x + by) % 4
        elif dim == "y":
            y = (y + by) % 4
        else:
            c = c ^ by
        return brick_of(zl, x, y, c)

    def permute(v, dim, by):
        return lax.ppermute(v, "brick", [(place[0], moved(place, dim, by)) for place in places()])

    value = value + permute(value, "core", 1)
    for dim in ("y", "x"):
        near = [permute(value, dim, by) for by in (1, 2, 3)]
        value = (value + near[0]) + (near[1] + near[2])
    pairs = {}
    for by in (1, 2, 3):
        table = []
        for brick, zl, x, y, c in places():
            for vec in range(2):
                z = (2 * vec + zl + by) % 4
                table.append((brick * 2 + vec, brick_of(z % 2, x, y, c) * 2 + z // 2))
        pairs[by] = table
    near = [lax.ppermute(value, ("brick", "vec"), pairs[by]) for by in (1, 2, 3)]
    value = (value + near[0]) + (near[1] + near[2])
    return value


def steps_of(levels, start_block):
    own_cols, planes, rows, lanes = start_block.shape
    bricks = lax.axis_size("brick")
    voxel_total = bricks * planes * rows * lanes
    halves = planes // 2
    upward = [(i, i + 1) for i in range(bricks - 1)]
    downward = [(i + 1, i) for i in range(bricks - 1)]
    swap = [(0, 1), (1, 0)]

    def up(value):
        return lax.ppermute(value, "brick", upward)

    def down(value):
        return lax.ppermute(value, "brick", downward)

    tail = pl.pallas_call(
        tail_kernel,
        out_shape=jax.ShapeDtypeStruct((sum(offsets_cube), rows, lanes), f32),
        in_specs=[HBM],
        out_specs=VMEM,
        scratch_shapes=[
            pltpu.VMEM((sum(offsets_cube), rows, lanes), jnp.int32),
            pltpu.SemaphoreType.DMA((len(offsets_cube),)),
        ],
        compiler_params=params(60),
        name="tail",
    )(levels)
    halo = up(tail)
    x_own = start_block.astype(f32)
    both = ("brick", "vec")
    x_relayed = []
    for half in range(2):
        direct, first_pairs, second_pairs = swap_tables(half)
        part = x_own[half * chunk : (half + 1) * chunk]
        part = lax.ppermute(part, both, first_pairs)
        x_relayed.append(lax.ppermute(part, both, second_pairs))
    x_other = lax.ppermute(x_own, both, direct)
    x_other = x_other + jnp.concatenate(x_relayed, axis=0)

    numbers = range(own_cols // chunk)
    edge = jax.ShapeDtypeStruct((chunk, deepest, rows, lanes), f32)
    root, *edges = pl.pallas_call(
        degree_kernel,
        out_shape=[jax.ShapeDtypeStruct((planes, rows, lanes), f32)] + [edge] * (2 * len(numbers)),
        in_specs=[VMEM] * 3,
        out_specs=[VMEM] * (1 + 2 * len(numbers)),
        compiler_params=params(4),
        name="degree",
    )(levels, halo, x_own)
    x_above, x_below = [], []
    for number in numbers:
        x_above.append(down(edges[2 * number]))
        x_below.append(up(edges[2 * number + 1]))

    terms = terms_of(rows, lanes)
    slots = len(terms)
    weights = pl.pallas_call(
        weights_kernel,
        out_shape=jax.ShapeDtypeStruct((slots, planes, rows, lanes), f32),
        in_specs=[VMEM] * 2,
        out_specs=VMEM,
        compiler_params=params(4),
        name="weights",
    )(levels, halo)
    ext = pltpu.VMEM((chunk, (planes + 2 * deepest) * rows, lanes), f32)

    def flat(value):
        return value.reshape(value.shape[0], -1, lanes)

    keep = jax.ShapeDtypeStruct(weights.shape, f32)

    def first_filter(number, weights):
        field = jax.ShapeDtypeStruct((chunk, planes, rows, lanes), f32)
        return pl.pallas_call(
            functools.partial(first_filter_kernel, number * chunk, terms, rows, lanes),
            out_shape=[field, edge, edge, keep],
            in_specs=[VMEM] * 5,
            out_specs=[VMEM] * 4,
            scratch_shapes=[ext],
            input_output_aliases={0: 3},
            compiler_params=params(8),
        )(weights, root, x_own, flat(x_below[number]), flat(x_above[number]))

    def second_filter(theirs, number, weights):
        return pl.pallas_call(
            functools.partial(second_filter_kernel, theirs, terms, rows, lanes),
            out_shape=[jax.ShapeDtypeStruct((chunk, halves, rows, lanes), f32), keep],
            in_specs=[VMEM] * 5,
            out_specs=[VMEM] * 2,
            scratch_shapes=[ext],
            input_output_aliases={0: 1},
            compiler_params=params(8),
        )(weights, root, fields[number], flat(belows[number]), flat(aboves[number]))

    fields, belows, aboves = [], [], []
    for number in numbers:
        field, low, high, weights = first_filter(number, weights)
        fields.append(field)
        aboves.append(down(low))
        belows.append(up(high))
    y_theirs, y_mine, y_other_mine = [], [], []
    for number in numbers:
        theirs, weights = second_filter(True, number, weights)
        y_theirs.append(theirs)
        y_other_mine.append(lax.ppermute(theirs, "vec", swap))
    for number in numbers:
        mine, weights = second_filter(False, number, weights)
        y_mine.append(mine)

    def tiled(value):
        return value.reshape(value.shape[0], -1, 8, lanes) if value.shape[2] != 8 else value

    mine_tiled = [tiled(value) for value in (x_own, x_other, *y_mine)]
    gram, outgoing = pl.pallas_call(
        gram_kernel,
        out_shape=(
            jax.ShapeDtypeStruct((2 * own_cols, 128), f32),
            jax.ShapeDtypeStruct((own_cols, halves * rows // 8, 8, lanes), f32),
        ),
        in_specs=[VMEM] * 6,
        out_specs=(VMEM, VMEM),
        scratch_shapes=[pltpu.VMEM((2, 256, 128), f32)],
        compiler_params=params(4),
        name="gram",
    )(*mine_tiled[:2], *map(tiled, y_theirs), *mine_tiled[2:])
    late = lax.ppermute(outgoing, "vec", [(0, 1)])
    gram = sum_everywhere(gram)

    small = jax.ShapeDtypeStruct((16, 16), f32)
    alpha, inverse, mix, project = pl.pallas_call(
        project_kernel,
        out_shape=[small, small, small, jax.ShapeDtypeStruct((2 * own_cols, 2 * own_cols, lanes), f32)],
        in_specs=[VMEM],
        out_specs=[VMEM] * 4,
        compiler_params=params(4),
        name="project",
    )(gram)
    rest_gram = pl.pallas_call(
        residual_kernel,
        out_shape=jax.ShapeDtypeStruct((2 * own_cols, 128), f32),
        in_specs=[VMEM] * 7,
        out_specs=VMEM,
        scratch_shapes=[
            pltpu.VMEM((2 * own_cols, halves * rows // 8, 8, lanes), f32),
            pltpu.VMEM((256, 128), f32),
        ],
        compiler_params=params(6),
        name="residual",
    )(project, *mine_tiled, *map(tiled, y_other_mine))
    rest_gram = sum_everywhere(rest_gram)
    beta, table = pl.pallas_call(
        functools.partial(algebra_kernel, math.sqrt(voxel_total)),
        out_shape=[small, jax.ShapeDtypeStruct((4 * own_cols, own_cols, lanes), f32)],
        in_specs=[VMEM] * 3,
        out_specs=[VMEM] * 2,
        compiler_params=params(4),
        name="algebra",
    )(rest_gram, inverse, mix)

    def combine(mine, *fields, before=None):
        half_tiles = halves * rows // 8
        extra = [] if before is None else [before]
        return pl.pallas_call(
            functools.partial(combine_kernel, mine),
            in_specs=[VMEM] * (1 + len(fields)) + [HBM] * len(extra),
            out_specs=HBM,
            out_shape=jax.ShapeDtypeStruct((own_cols, 2 * half_tiles, 8, lanes), f32),
            scratch_shapes=[
                pltpu.VMEM((own_cols, half_tiles, 8, lanes), f32),
                pltpu.SemaphoreType.DMA((half_tiles // 8,)),
            ],
            input_output_aliases={1 + len(fields): 0} if extra else {},
            compiler_params=params(4),
            name="combine_mine" if mine else "combine_theirs",
        )(table, *map(tiled, fields), *extra)

    basis = combine(True, x_own, x_other, *y_mine, *y_other_mine)
    basis = combine(False, x_own, x_other, *y_theirs, late, before=basis)
    return alpha[None], beta[None], basis.reshape(start_block.shape)


def solution(mesh):
    return jax.shard_map(
        steps_of,
        mesh=mesh,
        in_specs=(P(None, "brick", None, None), P("vec", "brick", None, None)),
        out_specs=(P(), P(), P("vec", "brick", None, None)),
        check_vma=False,
    )
```
